256 devices in a mesh: gx: 8 (over z_lo, x), gy: 32 (over z_hi, y, core).
Axes of the slice: x: 4, y: 4, z: 8 (z_hi: 4, z_lo: 2; z = z_hi * 2 + z_lo), core: 2. Of those that a mesh axis runs over, the one named last changes fastest.
Arguments:
- velocity: float32 [3, 32, 128, 4096], P(None, None, 'gx', 'gy'), may hold values from -6 to 6
- viscosity: float32 [32, 128, 4096], P(None, 'gx', 'gy'), may hold values from 0.02 to 0.12
- marker_cells: int32 [8192, 3, 128], P(('gx', 'gy')), may hold values from 0 to 4095, as said below
- marker_offset: float32 [8192, 3, 128], P(('gx', 'gy')), may hold values from 0 to 1
- marker_force: float32 [8192, 3, 128], P(('gx', 'gy')), may hold values from -24 to 24
Outputs:
- fluid_velocity: float32 [3, 32, 128, 4096], P(None, None, 'gx', 'gy')
- marker_velocity: float32 [8192, 3, 128], P(('gx', 'gy'))
The draws below stay inside these ranges and needn't reach their ends.
Inputs may be any that keep to these rules, and one draw needn't show every extreme that they name: `marker_cells`: within one block every marker's x lies in [i * 16, (i + 1) * 16) where i is the gx index of the device holding the block, every marker's y lies in one range [j * 128, (j + 1) * 128), and z lies in [1, 29]. One device holds at most 2 blocks whose y range is one given j, and in every gx column some j receives exactly 2 blocks from every device of that column.
All inputs are finite; a program needn't handle non-finite values.
Results may differ from the reference program's by a relative error of at most 0.0003.
The reference program's roundings to bfloat16 on the way count: a program that leaves them out, or rounds other values in their place, can miss the bound.
Values may be sent and summed in bfloat16 or wider, within the bound.
A program may use at most 128 MiB of HBM per device.

```python
import math
import jax
import jax.numpy as jnp
from jax import lax

CX = 16
CY = 128
NZ = 32
MARK = 128
BLK_DEV = 32
CAP = 2
NX = 128
NY = 4096
BLOCKS = 8192
N_GX = 8
N_GY = 32


def draw_marker_cells(key, part):
    keys = jax.random.split(key, 6)
    holders = N_GX * N_GY
    full_row = jax.random.randint(keys[0], (N_GX,), 0, N_GY)
    holder_column = jnp.arange(holders) // N_GY
    slot_index = jnp.arange(CAP * N_GY)
    slot_target = slot_index // CAP
    scores = jax.random.randint(keys[1], (holders, CAP * N_GY), 0, 2 ** 20) * (CAP * N_GY) + slot_index[None, :]
    scores = jnp.where(slot_target[None, :] == full_row[holder_column][:, None], -1 - slot_index[None, :], scores)
    picked = jnp.argsort(scores, axis=1, stable=True)[:, :BLK_DEV]
    targets = slot_target[picked]
    shuffle_scores = jax.random.randint(keys[2], (holders, BLK_DEV), 0, 2 ** 20) * BLK_DEV + jnp.arange(BLK_DEV)[None, :]
    shuffle = jnp.argsort(shuffle_scores, axis=1, stable=True)
    targets = jnp.take_along_axis(targets, shuffle, axis=1)
    x_cells = holder_column[:, None, None] * CX + jax.random.randint(keys[3], (holders, BLK_DEV, MARK), 0, CX)
    y_cells = targets[:, :, None] * CY + jax.random.randint(keys[4], (holders, BLK_DEV, MARK), 0, CY)
    z_cells = jax.random.randint(keys[5], (holders, BLK_DEV, MARK), 1, NZ - 2)
    stacked = jnp.stack([x_cells, y_cells, z_cells], axis=2)
    return stacked.reshape(holders * BLK_DEV, 3, MARK).astype(jnp.int32)


def levels(own_key, extent, cuts, low, high):
    gain, own = 1.0, jax.random.fold_in(own_key, 6)
    for axis_at, shards_of in cuts:
        heights = jnp.exp(jax.random.uniform(jax.random.fold_in(own, axis_at), (shards_of,), jnp.float32, low / len(cuts), high / len(cuts)))
        gain = gain * jnp.repeat(heights, extent[axis_at] // shards_of).reshape([-1 if axis == axis_at else 1 for axis in range(len(extent))])
    return gain


def gaussian(own_key, dims, width, bound, shards=(), kind=jnp.bfloat16):
    array = width * jax.random.normal(own_key, dims, jnp.float32)
    if shards:
        array = array * levels(own_key, dims, shards, -0.22, 0.18)
    return jnp.clip(array, -bound, bound).astype(kind)


def setup_inputs(seed: int = 0) -> dict:
    seeds = jax.random.split(jax.random.key(seed), 6)
    velocity = gaussian(seeds[0], (3, NZ, NX, NY), 1.0, 6.0, ((2, 8), (3, 32)), jnp.float32)
    viscosity = jnp.clip(jnp.exp(math.log(0.12) - 1.7917595 * jax.random.uniform(seeds[1], (NZ, NX, NY), jnp.float32) ** levels(seeds[1], (NZ, NX, NY), ((1, 8), (2, 32)), -0.2, 0.2)), 0.02, 0.12)
    marker_cells = draw_marker_cells(jax.random.fold_in(seeds[5], 71), 0)
    marker_offset = jnp.clip(1.0 * jax.random.uniform(seeds[3], (BLOCKS, 3, MARK), jnp.float32) ** levels(seeds[3], (BLOCKS, 3, MARK), ((0, 256),), -0.2, 0.2), 0.0, 1.0)
    marker_force = gaussian(seeds[4], (BLOCKS, 3, MARK), 4.0, 24.0, ((0, 256),), jnp.float32)
    return dict(velocity=velocity, viscosity=viscosity, marker_cells=marker_cells, marker_offset=marker_offset, marker_force=marker_force)


OFFSETS = (-1, 0, 1, 2)

def peskin_weight(distance):
    magnitude = jnp.abs(distance)
    inner = (3.0 - 2.0 * magnitude + jnp.sqrt(1.0 + 4.0 * magnitude - 4.0 * magnitude * magnitude)) / 8.0
    outer = (5.0 - 2.0 * magnitude - jnp.sqrt(-7.0 + 12.0 * magnitude - 4.0 * magnitude * magnitude)) / 8.0
    return jnp.where(magnitude < 1.0, inner, outer)

def relax_global(field, visc):

    def face(neighbor_field, neighbor_visc):
        return 0.5 * (visc + neighbor_visc) * (neighbor_field - field)
    total = face(jnp.roll(field, 1, axis=2), jnp.roll(visc, 1, axis=2))
    total = total + face(jnp.roll(field, -1, axis=2), jnp.roll(visc, -1, axis=2))
    total = total + face(jnp.roll(field, 1, axis=3), jnp.roll(visc, 1, axis=3))
    total = total + face(jnp.roll(field, -1, axis=3), jnp.roll(visc, -1, axis=3))
    vertical = field[:, 1:] - field[:, :-1]
    vertical = 0.5 * (visc[:, 1:] + visc[:, :-1]) * vertical
    zeros_layer = jnp.zeros_like(vertical[:, :1])
    z_term = jnp.concatenate([vertical, zeros_layer], axis=1) - jnp.concatenate([zeros_layer, vertical], axis=1)
    return field + (total + z_term)

def to_rounded(values):
    return lax.optimization_barrier(values.astype(jnp.bfloat16)).astype(jnp.float32)

def reference(velocity, viscosity, marker_cells, marker_offset, marker_force):
    cells = jnp.moveaxis(marker_cells, 1, 0).reshape(3, -1)
    offsets = jnp.moveaxis(marker_offset, 1, 0).reshape(3, -1)
    forces = jnp.moveaxis(marker_force, 1, 0).reshape(3, -1)
    weights = [[peskin_weight(shift_value - offsets[direction]) for shift_value in OFFSETS] for direction in range(3)]
    y_rounded = [to_rounded(weight_row) for weight_row in weights[1]]
    grid = jnp.zeros((3, NZ, NX, NY), jnp.float32)
    for z_place in range(4):
        z_cells = cells[2] + OFFSETS[z_place]
        for x_place in range(4):
            x_cells = (cells[0] + OFFSETS[x_place]) % NX
            lifted = to_rounded(forces * weights[2][z_place] * weights[0][x_place])
            for y_place in range(4):
                y_cells = (cells[1] + OFFSETS[y_place]) % NY
                grid = grid.at[:, z_cells, x_cells, y_cells].add(lifted * y_rounded[y_place])
    lifted_visc = viscosity[None]
    first_field = relax_global(velocity, lifted_visc)
    second_field = relax_global(first_field, lifted_visc)
    final_field = second_field + grid
    rounded_field = to_rounded(final_field)
    result = jnp.zeros((3, cells.shape[1]), jnp.float32)
    for z_place in range(4):
        z_cells = cells[2] + OFFSETS[z_place]
        for x_place in range(4):
            x_cells = (cells[0] + OFFSETS[x_place]) % NX
            partial_sum = jnp.zeros((3, cells.shape[1]), jnp.float32)
            for y_place in range(4):
                y_cells = (cells[1] + OFFSETS[y_place]) % NY
                partial_sum = partial_sum + rounded_field[:, z_cells, x_cells, y_cells] * y_rounded[y_place]
            result = result + partial_sum * weights[2][z_place] * weights[0][x_place]
    marker_velocity = jnp.moveaxis(result.reshape(3, BLOCKS, MARK), 0, 1)
    return (final_field, marker_velocity)
```

```python
import jax
import jax.numpy as jnp
from jax import lax
from jax.experimental import pallas as pl
from jax.experimental.pallas import tpu as pltpu
from jax.sharding import PartitionSpec as P

CAP = 2
OFFSETS = (-1, 0, 1, 2)
GROUP = 8
XR = 19
YR = 144


def peskin_weight(distance):
    magnitude = jnp.abs(distance)
    inner = (
        3.0 - 2.0 * magnitude + jnp.sqrt(1.0 + 4.0 * magnitude - 4.0 * magnitude * magnitude)
    ) / 8.0
    outer = (
        5.0 - 2.0 * magnitude - jnp.sqrt(-7.0 + 12.0 * magnitude - 4.0 * magnitude * magnitude)
    ) / 8.0
    return jnp.where(magnitude < 1.0, inner, outer)


def stencil_rows(rows, cell, weights, direction, slot, wrap):
    line = lax.broadcasted_iota(jnp.int32, (rows, cell.shape[1]), 0)
    matrix = jnp.zeros((rows, cell.shape[1]), jnp.float32)
    for place, shift in enumerate(OFFSETS):
        target = cell + shift
        if wrap:
            target = jnp.where(target < 0, rows - 1, target)
        matrix = jnp.where(
            line == target, weights[4 * direction + place, slot : slot + 1, :], matrix
        )
    return matrix


def spread_kernel(cells, weights, forces, total, y_out, x_out, z_out, lifted):
    depth = z_out.shape[1]
    markers = cells.shape[2]

    @pl.when(pl.program_id(0) == 0)
    def _():
        total[...] = jnp.zeros_like(total)

    for slot in range(GROUP):
        lanes = slice(slot * markers, (slot + 1) * markers)
        one = slice(slot, slot + 1)
        y_matrix = stencil_rows(YR, cells[1, one, :], weights, 1, slot, True)
        y_out[0, :, lanes] = y_matrix.astype(jnp.bfloat16)
        x_out[0, :, lanes] = stencil_rows(24, cells[0, one, :] + 1, weights, 0, slot, False)
        z_out[0, :, lanes] = stencil_rows(depth, cells[2, one, :], weights, 2, slot, False)
    for comp in range(3):
        for slot in range(GROUP):
            lanes = slice(slot * markers, (slot + 1) * markers)
            scaled = forces[comp, slot : slot + 1, :] * z_out[0, :, lanes]
            for x in range(XR):
                lifted[x * depth : (x + 1) * depth, lanes] = (
                    scaled * x_out[0, x : x + 1, lanes]
                ).astype(jnp.bfloat16)
        total[comp] += lax.dot_general(
            lifted[...], y_out[0], (((1,), (1,)), ((), ())), preferred_element_type=jnp.float32
        )


def sample_kernel(field, y_ref, x_ref, z_ref, out):
    depth = z_ref.shape[1]
    for comp in range(3):
        along_y = jnp.dot(field[comp], y_ref[0], preferred_element_type=jnp.float32)
        column = along_y[0:depth] * x_ref[0, 0:1, :]
        for x in range(1, XR):
            column = column + along_y[x * depth : (x + 1) * depth] * x_ref[0, x : x + 1, :]
        out[0, comp : comp + 1, :] = jnp.sum(column * z_ref[0], axis=0, keepdims=True)


def exchange(array, axis, dim, low_width, high_width):
    count, length = lax.axis_size(axis), array.shape[dim]
    up = [(i, (i + 1) % count) for i in range(count)]
    down = [(j, i) for i, j in up]
    before = lax.ppermute(
        lax.slice_in_dim(array, length - low_width, length, axis=dim), axis, up
    )
    after = lax.ppermute(lax.slice_in_dim(array, 0, high_width, axis=dim), axis, down)
    return before, after


def padded(array, axis, dim, width):
    before, after = exchange(array, axis, dim, width, width)
    return jnp.concatenate([before, array, after], axis=dim)


def relax(field, visc):
    center_field = field[:, 1:-1, :, 1:-1]
    center_visc = visc[:, 1:-1, :, 1:-1]

    def face(neighbor_field, neighbor_visc):
        return 0.5 * (center_visc + neighbor_visc) * (neighbor_field - center_field)

    total = face(field[:, :-2, :, 1:-1], visc[:, :-2, :, 1:-1])
    total = total + face(field[:, 2:, :, 1:-1], visc[:, 2:, :, 1:-1])
    total = total + face(field[:, 1:-1, :, :-2], visc[:, 1:-1, :, :-2])
    total = total + face(field[:, 1:-1, :, 2:], visc[:, 1:-1, :, 2:])
    vertical = center_field[:, :, 1:] - center_field[:, :, :-1]
    vertical = 0.5 * (center_visc[:, :, 1:] + center_visc[:, :, :-1]) * vertical
    zeros_layer = jnp.zeros_like(vertical[:, :, :1])
    z_term = jnp.concatenate([vertical, zeros_layer], axis=2) - jnp.concatenate(
        [zeros_layer, vertical], axis=2
    )
    return center_field + (total + z_term)


def body(velocity, viscosity, marker_cells, marker_offset, marker_force):
    depth, width_x, width_y = velocity.shape[1:]
    blocks, _, markers = marker_cells.shape
    column_size = lax.axis_size("gy")
    slots = column_size * CAP
    steps = slots // GROUP

    target = marker_cells[:, 1, 0] // width_y
    same = target[:, None] == target[None, :]
    earlier = jnp.tril(jnp.ones((blocks, blocks), jnp.bool_), -1)
    rank = jnp.sum(jnp.where(same & earlier, 1, 0), axis=1)
    slot_of = target * CAP + rank
    place = (lax.broadcasted_iota(jnp.int32, (slots, blocks), 0) == slot_of[None, :]).astype(
        jnp.float32
    )
    local = jnp.stack(
        [
            marker_cells[:, 0] - lax.axis_index("gx") * width_x,
            marker_cells[:, 1] - target[:, None] * width_y,
            marker_cells[:, 2],
        ],
        axis=1,
    )
    packed = jnp.concatenate([local.astype(jnp.float32), marker_offset, marker_force], axis=1)
    sent = jnp.dot(place, packed.reshape(blocks, -1), precision=lax.Precision.HIGHEST)
    sent = sent.reshape(column_size, CAP * 9, markers)
    received = lax.all_to_all(sent, "gy", 0, 0, tiled=True)
    received = jnp.moveaxis(received.reshape(slots, 9, markers), 1, 0)
    cells = received[0:3].astype(jnp.int32)
    weights = jnp.stack(
        [peskin_weight(shift - received[3 + d]) for d in range(3) for shift in OFFSETS]
    )
    forces = received[6:9]

    rows = XR * depth
    lanes = GROUP * markers
    total, y_matrix, x_matrix, z_matrix = pl.pallas_call(
        spread_kernel,
        grid=(steps,),
        in_specs=[
            pl.BlockSpec((3, GROUP, markers), lambda g: (0, g, 0)),
            pl.BlockSpec((12, GROUP, markers), lambda g: (0, g, 0)),
            pl.BlockSpec((3, GROUP, markers), lambda g: (0, g, 0)),
        ],
        out_specs=[
            pl.BlockSpec((3, rows, YR), lambda g: (0, 0, 0)),
            pl.BlockSpec((1, YR, lanes), lambda g: (g, 0, 0)),
            pl.BlockSpec((1, 24, lanes), lambda g: (g, 0, 0)),
            pl.BlockSpec((1, depth, lanes), lambda g: (g, 0, 0)),
        ],
        out_shape=[
            jax.ShapeDtypeStruct((3, rows, YR), jnp.float32),
            jax.ShapeDtypeStruct((steps, YR, lanes), jnp.bfloat16),
            jax.ShapeDtypeStruct((steps, 24, lanes), jnp.float32),
            jax.ShapeDtypeStruct((steps, depth, lanes), jnp.float32),
        ],
        scratch_shapes=[pltpu.VMEM((rows, lanes), jnp.bfloat16)],
        name="spread",
    )(cells, weights, forces)

    stacked = jnp.concatenate([velocity, viscosity[None]], axis=0)
    stacked = jnp.swapaxes(stacked, 1, 2)
    stacked = padded(padded(stacked, "gx", 1, 2), "gy", 3, 2)
    visc = stacked[3:4]
    first = relax(stacked[0:3], visc)
    second = relax(first, visc[:, 1:-1, :, 1:-1])

    total = total.reshape(3, XR, depth, YR)
    count_x, count_y = lax.axis_size("gx"), lax.axis_size("gy")
    up_x = [(i, (i + 1) % count_x) for i in range(count_x)]
    down_x = [(j, i) for i, j in up_x]
    up_y = [(i, (i + 1) % count_y) for i in range(count_y)]
    down_y = [(j, i) for i, j in up_y]
    from_low = lax.ppermute(total[:, width_x + 1 :], "gx", up_x)
    from_high = lax.ppermute(total[:, 0:1], "gx", down_x)
    core = total[:, 1 : width_x + 1]
    core = core + jnp.pad(from_low, ((0, 0), (0, width_x - 2), (0, 0), (0, 0)))
    core = core + jnp.pad(from_high, ((0, 0), (width_x - 1, 0), (0, 0), (0, 0)))
    from_low = lax.ppermute(core[..., width_y : width_y + 2], "gy", up_y)
    from_high = lax.ppermute(core[..., YR - 1 :], "gy", down_y)
    force = core[..., :width_y]
    force = force + jnp.pad(from_low, ((0, 0), (0, 0), (0, 0), (0, width_y - 2)))
    force = force + jnp.pad(from_high, ((0, 0), (0, 0), (0, 0), (width_y - 1, 0)))
    final = second + force

    rounded = final.astype(jnp.bfloat16)
    before, after = exchange(rounded, "gx", 1, 1, 2)
    rounded = jnp.concatenate([before, rounded, after], axis=1)
    before, after = exchange(rounded, "gy", 3, 1, 2)
    middle = jnp.zeros((3, XR, depth, YR - width_y - 3), jnp.bfloat16)
    field = jnp.concatenate([rounded, after, middle, before], axis=3).reshape(3, rows, YR)

    sampled = pl.pallas_call(
        sample_kernel,
        grid=(steps,),
        in_specs=[
            pl.BlockSpec((3, rows, YR), lambda g: (0, 0, 0)),
            pl.BlockSpec((1, YR, lanes), lambda g: (g, 0, 0)),
            pl.BlockSpec((1, 24, lanes), lambda g: (g, 0, 0)),
            pl.BlockSpec((1, depth, lanes), lambda g: (g, 0, 0)),
        ],
        out_specs=pl.BlockSpec((1, 3, lanes), lambda g: (g, 0, 0)),
        out_shape=jax.ShapeDtypeStruct((steps, 3, lanes), jnp.float32),
        name="sample",
    )(field, y_matrix, x_matrix, z_matrix)
    sampled = jnp.swapaxes(sampled.reshape(steps, 3, GROUP, markers), 1, 2)
    sampled = sampled.reshape(column_size, CAP * 3, markers)
    returned = lax.all_to_all(sampled, "gy", 0, 0, tiled=True).reshape(slots, -1)
    marker_velocity = jnp.dot(place.T, returned, precision=lax.Precision.HIGHEST)
    return (jnp.swapaxes(final, 1, 2), marker_velocity.reshape(blocks, 3, markers))


def solution(mesh):
    in_specs = (
        P(None, None, "gx", "gy"),
        P(None, "gx", "gy"),
        P(("gx", "gy"), None, None),
        P(("gx", "gy"), None, None),
        P(("gx", "gy"), None, None),
    )
    out_specs = (P(None, None, "gx", "gy"), P(("gx", "gy"), None, None))
    return jax.shard_map(body, mesh=mesh, in_specs=in_specs, out_specs=out_specs, check_vma=False)
```

```python
import functools

import jax
import jax.numpy as jnp
from jax import lax
from jax.experimental import pallas as pl
from jax.experimental.pallas import tpu as pltpu
from jax.sharding import PartitionSpec as P

CAP = 2
OFFSETS = (-1, 0, 1, 2)
GROUP = 8
XR = 19
YR = 144


def peskin_weight(distance):
    magnitude = jnp.abs(distance)
    inner = (
        3.0 - 2.0 * magnitude + jnp.sqrt(1.0 + 4.0 * magnitude - 4.0 * magnitude * magnitude)
    ) / 8.0
    outer = (
        5.0 - 2.0 * magnitude - jnp.sqrt(-7.0 + 12.0 * magnitude - 4.0 * magnitude * magnitude)
    ) / 8.0
    return jnp.where(magnitude < 1.0, inner, outer)


def stencil_rows(rows, cell, weights, direction, slot, wrap):
    line = lax.broadcasted_iota(jnp.int32, (rows, cell.shape[1]), 0)
    matrix = jnp.zeros((rows, cell.shape[1]), jnp.float32)
    for place, shift in enumerate(OFFSETS):
        target = cell + shift
        if wrap:
            target = jnp.where(target < 0, rows - 1, target)
        matrix = jnp.where(
            line == target, weights[4 * direction + place, slot : slot + 1, :], matrix
        )
    return matrix


def spread_kernel(
    cells, weights, forces, core, above, below, y_out, x_out, z_out, lifted, total
):
    depth = z_out.shape[1]
    markers = cells.shape[2]
    rows = lifted.shape[0]

    @pl.when(pl.program_id(0) == 0)
    def _():
        total[...] = jnp.zeros_like(total)

    for slot in range(GROUP):
        lanes = slice(slot * markers, (slot + 1) * markers)
        one = slice(slot, slot + 1)
        y_matrix = stencil_rows(YR, cells[1, one, :], weights, 1, slot, True)
        y_out[0, :, lanes] = y_matrix.astype(jnp.bfloat16)
        x_out[0, :, lanes] = stencil_rows(24, cells[0, one, :] + 1, weights, 0, slot, False)
        z_out[0, :, lanes] = stencil_rows(depth, cells[2, one, :], weights, 2, slot, False)
    for comp in range(3):
        for slot in range(GROUP):
            lanes = slice(slot * markers, (slot + 1) * markers)
            scaled = forces[comp, slot : slot + 1, :] * z_out[0, :, lanes]
            for x in range(XR):
                lifted[x * depth : (x + 1) * depth, lanes] = (
                    scaled * x_out[0, x : x + 1, lanes]
                ).astype(jnp.bfloat16)
        total[comp, 0:rows, 0:YR] += lax.dot_general(
            lifted[...], y_out[0], (((1,), (1,)), ((), ())), preferred_element_type=jnp.float32
        )

    @pl.when(pl.program_id(0) == pl.num_programs(0) - 1)
    def _():
        for comp in range(3):
            core[comp] = total[comp, :, 0:128]
            for tile in range(5):
                turned = total[comp, tile * 128 : (tile + 1) * 128, 128:256].T
                above[comp, tile] = turned[0:8]
                below[comp, tile] = turned[8:16]


def sample_kernel(field, y_ref, x_ref, z_ref, out):
    depth = z_ref.shape[1]
    for comp in range(3):
        along_y = jnp.dot(
            field[comp, 0 : XR * depth, 0:YR], y_ref[0], preferred_element_type=jnp.float32
        )
        column = along_y[0:depth] * x_ref[0, 0:1, :]
        for x in range(1, XR):
            column = column + along_y[x * depth : (x + 1) * depth] * x_ref[0, x : x + 1, :]
        out[0, comp : comp + 1, :] = jnp.sum(column * z_ref[0], axis=0, keepdims=True)


def settle_kernel(
    count_x, count_y, stacked, core, above, below,
    final, field,
    wide, first, force, rim, from_low_y, from_high_y, from_low_x, from_high_x,
    to_high, to_low, ghost_low, ghost_high, rim_up, rim_down, rim_low, rim_high,
    send_sems, recv_sems,
):
    me_x, me_y = lax.axis_index("gx"), lax.axis_index("gy")
    up_x = (lax.rem(me_x + 1, count_x), me_y)
    down_x = (lax.rem(me_x + count_x - 1, count_x), me_y)
    up_y = (me_x, lax.rem(me_y + 1, count_y))
    down_y = (me_x, lax.rem(me_y + count_y - 1, count_y))

    barrier = pltpu.get_barrier_semaphore()
    for device in (up_x, down_x, up_y, down_y):
        pl.semaphore_signal(barrier, inc=1, device_id=device, device_id_type=pl.DeviceIdType.MESH)
    pl.semaphore_wait(barrier, 4)

    def send(number, source, target, device):
        copy = pltpu.make_async_remote_copy(
            src_ref=source,
            dst_ref=target,
            send_sem=send_sems.at[number],
            recv_sem=recv_sems.at[number],
            device_id=device,
            device_id_type=pl.DeviceIdType.MESH,
        )
        copy.start()
        return copy

    def tiles(comps, body):
        def step(index, carry):
            body(index // 5, lax.rem(index, 5))
            return carry

        lax.fori_loop(0, comps * 5, step, 0)

    x_up = send(0, stacked.at[:, 14:16], wide.at[:, 0:2, :, 0:128], up_x)
    x_down = send(1, stacked.at[:, 0:2], wide.at[:, 18:20, :, 0:128], down_x)
    y_up = send(2, above, from_low_y, up_y)
    y_down = send(3, below, from_high_y, down_y)

    wide[:, 2:18, :, 0:128] = stacked[...]
    rim[:, 19:20] = jnp.zeros_like(rim[:, 19:20])
    x_up.wait()
    x_down.wait()

    def turn_wide(comp, tile):
        turned = wide[comp, pl.ds(4 * tile, 4), :, 0:128].reshape(128, 128).T
        to_low[comp, tile] = turned[0:8]
        to_high[comp, tile] = turned[120:128]

    tiles(4, turn_wide)
    wide_up = send(4, to_high, ghost_low, up_y)
    wide_down = send(5, to_low, ghost_high, down_y)
    y_up.wait()
    y_down.wait()

    def add_force(comp, tile):
        middle = jnp.zeros((112, 128), jnp.float32)
        turned = jnp.concatenate(
            [from_low_y[comp, tile], middle, from_high_y[comp, tile]], axis=0
        ).T
        part = pl.ds(4 * tile, 4)
        force[comp, part] = core[comp, part] + turned.reshape(4, 32, 128)

    tiles(3, add_force)
    force_up = send(6, force.at[:, 17:19], from_low_x, up_x)
    force_down = send(7, force.at[:, 0:1], from_high_x, down_x)
    wide_up.wait()
    wide_down.wait()

    def fill_wide(comp, tile):
        middle = jnp.zeros((112, 128), jnp.float32)
        turned = jnp.concatenate(
            [ghost_high[comp, tile], middle, ghost_low[comp, tile]], axis=0
        ).T
        wide[comp, pl.ds(4 * tile, 4), :, 128:256] = turned.reshape(4, 32, 128)

    tiles(4, fill_wide)

    height = lax.broadcasted_iota(jnp.int32, (32, 256), 0)

    def relaxed(source, x, visc_x, store):
        visc = wide[3, visc_x]
        low_x = 0.5 * (visc + wide[3, visc_x - 1])
        high_x = 0.5 * (visc + wide[3, visc_x + 1])
        low_y = 0.5 * (visc + pltpu.roll(visc, 1, 1))
        high_y = 0.5 * (visc + pltpu.roll(visc, 255, 1))
        low_z = jnp.where(height > 0, 0.5 * (visc + pltpu.roll(visc, 1, 0)), 0.0)
        high_z = jnp.where(height < 31, 0.5 * (visc + pltpu.roll(visc, 31, 0)), 0.0)
        for comp in range(3):
            here = source[comp, x]
            total = low_x * (source[comp, x - 1] - here)
            total = total + high_x * (source[comp, x + 1] - here)
            total = total + low_y * (pltpu.roll(here, 1, 1) - here)
            total = total + high_y * (pltpu.roll(here, 255, 1) - here)
            total = total + low_z * (pltpu.roll(here, 1, 0) - here)
            total = total + high_z * (pltpu.roll(here, 31, 0) - here)
            store(comp, here + total)

    def first_step(x, carry):
        def store(comp, value):
            first[comp, x - 1] = value

        relaxed(wide, x, x, store)
        return carry

    lax.fori_loop(1, 19, first_step, 0)

    force_up.wait()
    force_down.wait()
    force[:, 1:3] = force[:, 1:3] + from_low_x[...]
    force[:, 16:17] = force[:, 16:17] + from_high_x[...]

    def second_step(x, carry):
        def store(comp, value):
            total = value[:, 0:128] + force[comp, x]
            final[comp, x - 1] = total
            rim[comp, x] = total.astype(jnp.bfloat16)

        relaxed(first, x, x + 1, store)
        return carry

    lax.fori_loop(1, 17, second_step, 0)

    rim_x_up = send(8, rim.at[:, 16:17], rim.at[:, 0:1], up_x)
    rim_x_down = send(9, rim.at[:, 1:3], rim.at[:, 17:19], down_x)
    rim_x_up.wait()
    rim_x_down.wait()

    def turn_rim(comp, tile):
        part = pl.ds(4 * tile, 4)
        rows = rim[comp, part]
        field[comp, part, :, 0:128] = rows
        turned = rows.astype(jnp.float32).reshape(128, 128).T
        rim_down[comp, tile] = turned[0:8]
        rim_up[comp, tile] = turned[120:128]

    tiles(3, turn_rim)
    rim_y_up = send(10, rim_up, rim_low, up_y)
    rim_y_down = send(11, rim_down, rim_high, down_y)
    rim_y_up.wait()
    rim_y_down.wait()

    def fill_field(comp, tile):
        rest = jnp.zeros((112, 128), jnp.float32)
        turned = jnp.concatenate([rim_high[comp, tile], rim_low[comp, tile], rest], axis=0).T
        field[comp, pl.ds(4 * tile, 4), :, 128:256] = turned.reshape(4, 32, 128).astype(
            jnp.bfloat16
        )

    tiles(3, fill_field)


def settle(stacked, core, above, below):
    vmem = pl.BlockSpec(memory_space=pltpu.VMEM)

    def ghosts(comps):
        return pltpu.VMEM((comps, 5, 8, 128), jnp.float32)

    return pl.pallas_call(
        functools.partial(settle_kernel, lax.axis_size("gx"), lax.axis_size("gy")),
        in_specs=[vmem] * 4,
        out_specs=[vmem] * 2,
        out_shape=[
            jax.ShapeDtypeStruct((3, 16, 32, 128), jnp.float32),
            jax.ShapeDtypeStruct((3, 20, 32, 256), jnp.bfloat16),
        ],
        scratch_shapes=[
            pltpu.VMEM((4, 20, 32, 256), jnp.float32),
            pltpu.VMEM((3, 18, 32, 256), jnp.float32),
            pltpu.VMEM((3, 20, 32, 128), jnp.float32),
            pltpu.VMEM((3, 20, 32, 128), jnp.bfloat16),
            ghosts(3),
            ghosts(3),
            pltpu.VMEM((3, 2, 32, 128), jnp.float32),
            pltpu.VMEM((3, 1, 32, 128), jnp.float32),
            ghosts(4),
            ghosts(4),
            ghosts(4),
            ghosts(4),
            ghosts(3),
            ghosts(3),
            ghosts(3),
            ghosts(3),
            pltpu.SemaphoreType.DMA((12,)),
            pltpu.SemaphoreType.DMA((12,)),
        ],
        compiler_params=pltpu.CompilerParams(
            collective_id=0, has_side_effects=True, vmem_limit_bytes=40 * 2**20
        ),
        name="settle",
    )(stacked, core, above, below)


def body(velocity, viscosity, marker_cells, marker_offset, marker_force):
    depth, width_x, width_y = velocity.shape[1:]
    blocks, _, markers = marker_cells.shape
    column_size = lax.axis_size("gy")
    slots = column_size * CAP
    steps = slots // GROUP

    target = marker_cells[:, 1, 0] // width_y
    same = target[:, None] == target[None, :]
    earlier = jnp.tril(jnp.ones((blocks, blocks), jnp.bool_), -1)
    rank = jnp.sum(jnp.where(same & earlier, 1, 0), axis=1)
    slot_of = target * CAP + rank
    place = (lax.broadcasted_iota(jnp.int32, (slots, blocks), 0) == slot_of[None, :]).astype(
        jnp.float32
    )
    local = jnp.stack(
        [
            marker_cells[:, 0] - lax.axis_index("gx") * width_x,
            marker_cells[:, 1] - target[:, None] * width_y,
            marker_cells[:, 2],
        ],
        axis=1,
    )
    packed = jnp.concatenate([local.astype(jnp.float32), marker_offset, marker_force], axis=1)
    sent = jnp.dot(place, packed.reshape(blocks, -1), precision=lax.Precision.HIGHEST)
    sent = sent.reshape(column_size, CAP * 9, markers)
    received = lax.all_to_all(sent, "gy", 0, 0, tiled=True)
    received = jnp.moveaxis(received.reshape(slots, 9, markers), 1, 0)
    cells = received[0:3].astype(jnp.int32)
    weights = jnp.stack(
        [peskin_weight(shift - received[3 + d]) for d in range(3) for shift in OFFSETS]
    )
    forces = received[6:9]

    rows = XR * depth
    lanes = GROUP * markers
    core, above, below, y_matrix, x_matrix, z_matrix = pl.pallas_call(
        spread_kernel,
        grid=(steps,),
        in_specs=[
            pl.BlockSpec((3, GROUP, markers), lambda g: (0, g, 0)),
            pl.BlockSpec((12, GROUP, markers), lambda g: (0, g, 0)),
            pl.BlockSpec((3, GROUP, markers), lambda g: (0, g, 0)),
        ],
        out_specs=[
            pl.BlockSpec((3, 640, 128), lambda g: (0, 0, 0)),
            pl.BlockSpec((3, 5, 8, 128), lambda g: (0, 0, 0, 0)),
            pl.BlockSpec((3, 5, 8, 128), lambda g: (0, 0, 0, 0)),
            pl.BlockSpec((1, YR, lanes), lambda g: (g, 0, 0)),
            pl.BlockSpec((1, 24, lanes), lambda g: (g, 0, 0)),
            pl.BlockSpec((1, depth, lanes), lambda g: (g, 0, 0)),
        ],
        out_shape=[
            jax.ShapeDtypeStruct((3, 640, 128), jnp.float32),
            jax.ShapeDtypeStruct((3, 5, 8, 128), jnp.float32),
            jax.ShapeDtypeStruct((3, 5, 8, 128), jnp.float32),
            jax.ShapeDtypeStruct((steps, YR, lanes), jnp.bfloat16),
            jax.ShapeDtypeStruct((steps, 24, lanes), jnp.float32),
            jax.ShapeDtypeStruct((steps, depth, lanes), jnp.float32),
        ],
        scratch_shapes=[
            pltpu.VMEM((rows, lanes), jnp.bfloat16),
            pltpu.VMEM((3, 640, 256), jnp.float32),
        ],
        name="spread",
    )(cells, weights, forces)

    stacked = jnp.concatenate([velocity, viscosity[None]], axis=0)
    stacked = jnp.swapaxes(stacked, 1, 2)
    final, field = settle(stacked, core.reshape(3, 20, depth, width_y), above, below)
    field = field.reshape(3, 640, 256)

    sampled = pl.pallas_call(
        sample_kernel,
        grid=(steps,),
        in_specs=[
            pl.BlockSpec((3, 640, 256), lambda g: (0, 0, 0)),
            pl.BlockSpec((1, YR, lanes), lambda g: (g, 0, 0)),
            pl.BlockSpec((1, 24, lanes), lambda g: (g, 0, 0)),
            pl.BlockSpec((1, depth, lanes), lambda g: (g, 0, 0)),
        ],
        out_specs=pl.BlockSpec((1, 3, lanes), lambda g: (g, 0, 0)),
        out_shape=jax.ShapeDtypeStruct((steps, 3, lanes), jnp.float32),
        name="sample",
    )(field, y_matrix, x_matrix, z_matrix)
    sampled = jnp.swapaxes(sampled.reshape(steps, 3, GROUP, markers), 1, 2)
    sampled = sampled.reshape(column_size, CAP * 3, markers)
    returned = lax.all_to_all(sampled, "gy", 0, 0, tiled=True).reshape(slots, -1)
    marker_velocity = jnp.dot(place.T, returned, precision=lax.Precision.HIGHEST)
    return (jnp.swapaxes(final, 1, 2), marker_velocity.reshape(blocks, 3, markers))


def solution(mesh):
    in_specs = (
        P(None, None, "gx", "gy"),
        P(None, "gx", "gy"),
        P(("gx", "gy"), None, None),
        P(("gx", "gy"), None, None),
        P(("gx", "gy"), None, None),
    )
    out_specs = (P(None, None, "gx", "gy"), P(("gx", "gy"), None, None))
    return jax.shard_map(body, mesh=mesh, in_specs=in_specs, out_specs=out_specs, check_vma=False)
```

```python
import functools

import jax
import jax.numpy as jnp
from jax import lax
from jax.experimental import pallas as pl
from jax.experimental.pallas import tpu as pltpu
from jax.sharding import PartitionSpec as P

CAP = 2
OFFSETS = (-1, 0, 1, 2)
GROUP = 8
XR = 19
YR = 144


def peskin_weight(distance):
    magnitude = jnp.abs(distance)
    inner = (
        3.0 - 2.0 * magnitude + jnp.sqrt(1.0 + 4.0 * magnitude - 4.0 * magnitude * magnitude)
    ) / 8.0
    outer = (
        5.0 - 2.0 * magnitude - jnp.sqrt(-7.0 + 12.0 * magnitude - 4.0 * magnitude * magnitude)
    ) / 8.0
    return jnp.where(magnitude < 1.0, inner, outer)


def stencil_rows(rows, cell, weights, direction, slot, wrap):
    line = lax.broadcasted_iota(jnp.int32, (rows, cell.shape[1]), 0)
    matrix = jnp.zeros((rows, cell.shape[1]), jnp.float32)
    for place, shift in enumerate(OFFSETS):
        target = cell + shift
        if wrap:
            target = jnp.where(target < 0, rows - 1, target)
        matrix = jnp.where(
            line == target, weights[4 * direction + place, slot : slot + 1, :], matrix
        )
    return matrix


def spread_kernel(
    cells, weights, forces, core, above, below, y_out, x_out, z_out, lifted, total
):
    depth = z_out.shape[1]
    markers = cells.shape[3]
    rows = lifted.shape[0]
    step = pl.program_id(0)
    cells, weights, forces = cells.at[:, step], weights.at[:, step], forces.at[:, step]

    @pl.when(pl.program_id(0) == 0)
    def _():
        total[...] = jnp.zeros_like(total)

    for slot in range(GROUP):
        lanes = slice(slot * markers, (slot + 1) * markers)
        one = slice(slot, slot + 1)
        y_matrix = stencil_rows(YR, cells[1, one, :], weights, 1, slot, True)
        y_out[0, :, lanes] = y_matrix.astype(jnp.bfloat16)
        x_out[0, :, lanes] = stencil_rows(24, cells[0, one, :] + 1, weights, 0, slot, False)
        z_out[0, :, lanes] = stencil_rows(depth, cells[2, one, :], weights, 2, slot, False)
    for comp in range(3):
        for slot in range(GROUP):
            lanes = slice(slot * markers, (slot + 1) * markers)
            scaled = forces[comp, slot : slot + 1, :] * z_out[0, :, lanes]
            for x in range(XR):
                lifted[x * depth : (x + 1) * depth, lanes] = (
                    scaled * x_out[0, x : x + 1, lanes]
                ).astype(jnp.bfloat16)
        total[comp, 0:rows, 0:YR] += lax.dot_general(
            lifted[...], y_out[0], (((1,), (1,)), ((), ())), preferred_element_type=jnp.float32
        )

    @pl.when(pl.program_id(0) == pl.num_programs(0) - 1)
    def _():
        for comp in range(3):
            core[comp] = total[comp, :, 0:128]
            for tile in range(5):
                turned = total[comp, tile * 128 : (tile + 1) * 128, 128:256].T
                above[comp, tile] = turned[0:8]
                below[comp, tile] = turned[8:16]


def sample_kernel(field, y_ref, x_ref, z_ref, out):
    depth = z_ref.shape[1]
    for comp in range(3):
        along_y = jnp.dot(
            field[comp, 0 : XR * depth, 0:YR], y_ref[0], preferred_element_type=jnp.float32
        )
        column = along_y[0:depth] * x_ref[0, 0:1, :]
        for x in range(1, XR):
            column = column + along_y[x * depth : (x + 1) * depth] * x_ref[0, x : x + 1, :]
        result = jnp.sum(column * z_ref[0], axis=0, keepdims=True)
        for slot in range(GROUP):
            row = (slot % CAP) * 3 + comp
            out[slot // CAP, row : row + 1, :] = result[:, slot * 128 : (slot + 1) * 128]


MESH = pl.DeviceIdType.MESH


def neighbours(count_x, count_y):
    me_x, me_y = lax.axis_index("gx"), lax.axis_index("gy")
    up_x = (lax.rem(me_x + 1, count_x), me_y)
    down_x = (lax.rem(me_x + count_x - 1, count_x), me_y)
    up_y = (me_x, lax.rem(me_y + 1, count_y))
    down_y = (me_x, lax.rem(me_y + count_y - 1, count_y))
    return up_x, down_x, up_y, down_y


def greet(devices):
    barrier = pltpu.get_barrier_semaphore()
    for device in devices:
        pl.semaphore_signal(barrier, inc=1, device_id=device, device_id_type=MESH)
    pl.semaphore_wait(barrier, len(devices))


def sender(send_sems, recv_sems):
    def send(number, source, target, device):
        copy = pltpu.make_async_remote_copy(
            src_ref=source,
            dst_ref=target,
            send_sem=send_sems.at[number],
            recv_sem=recv_sems.at[number],
            device_id=device,
            device_id_type=MESH,
        )
        copy.start()
        return copy

    return send


def tiles(comps, body):
    def step(index, carry):
        body(index // 5, lax.rem(index, 5))
        return carry

    lax.fori_loop(0, comps * 5, step, 0)


def flow_kernel(
    count_x, count_y, stacked, second, wide, first, to_high, to_low, ghost_low, ghost_high,
    send_sems, recv_sems,
):
    up_x, down_x, up_y, down_y = neighbours(count_x, count_y)
    greet((up_x, down_x, up_y, down_y))
    send = sender(send_sems, recv_sems)
    x_up = send(0, stacked.at[:, 14:16], wide.at[:, 0:2, :, 0:128], up_x)
    x_down = send(1, stacked.at[:, 0:2], wide.at[:, 18:20, :, 0:128], down_x)
    wide[:, 2:18, :, 0:128] = stacked[...]
    x_up.wait()
    x_down.wait()

    def turn_wide(comp, tile):
        turned = wide[comp, pl.ds(4 * tile, 4), :, 0:128].reshape(128, 128).T
        to_low[comp, tile] = turned[0:8]
        to_high[comp, tile] = turned[120:128]

    tiles(4, turn_wide)
    wide_up = send(2, to_high, ghost_low, up_y)
    wide_down = send(3, to_low, ghost_high, down_y)
    wide_up.wait()
    wide_down.wait()

    def fill_wide(comp, tile):
        middle = jnp.zeros((112, 128), jnp.float32)
        turned = jnp.concatenate(
            [ghost_high[comp, tile], middle, ghost_low[comp, tile]], axis=0
        ).T
        wide[comp, pl.ds(4 * tile, 4), :, 128:256] = turned.reshape(4, 32, 128)

    tiles(4, fill_wide)

    height = lax.broadcasted_iota(jnp.int32, (32, 256), 0)

    def relaxed(source, x, visc_x, store):
        visc = wide[3, visc_x]
        low_x = 0.5 * (visc + wide[3, visc_x - 1])
        high_x = 0.5 * (visc + wide[3, visc_x + 1])
        low_y = 0.5 * (visc + pltpu.roll(visc, 1, 1))
        high_y = 0.5 * (visc + pltpu.roll(visc, 255, 1))
        low_z = jnp.where(height > 0, 0.5 * (visc + pltpu.roll(visc, 1, 0)), 0.0)
        high_z = jnp.where(height < 31, 0.5 * (visc + pltpu.roll(visc, 31, 0)), 0.0)
        for comp in range(3):
            here = source[comp, x]
            total = low_x * (source[comp, x - 1] - here)
            total = total + high_x * (source[comp, x + 1] - here)
            total = total + low_y * (pltpu.roll(here, 1, 1) - here)
            total = total + high_y * (pltpu.roll(here, 255, 1) - here)
            total = total + low_z * (pltpu.roll(here, 1, 0) - here)
            total = total + high_z * (pltpu.roll(here, 31, 0) - here)
            store(comp, here + total)

    def first_step(x, carry):
        def store(comp, value):
            first[comp, x - 1] = value

        relaxed(wide, x, x, store)
        return carry

    lax.fori_loop(1, 19, first_step, 0)

    def second_step(x, carry):
        def store(comp, value):
            second[comp, x - 1] = value[:, 0:128]

        relaxed(first, x, x + 1, store)
        return carry

    lax.fori_loop(1, 17, second_step, 0)


def settle_kernel(
    count_x, count_y, second, core, above, below,
    final, field,
    force, rim, from_low_y, from_high_y, from_low_x, from_high_x,
    rim_up, rim_down, rim_low, rim_high, send_sems, recv_sems,
):
    up_x, down_x, up_y, down_y = neighbours(count_x, count_y)
    greet((up_x, down_x, up_y, down_y))
    send = sender(send_sems, recv_sems)
    y_up = send(0, above, from_low_y, up_y)
    y_down = send(1, below, from_high_y, down_y)
    rim[:, 19:20] = jnp.zeros_like(rim[:, 19:20])
    y_up.wait()
    y_down.wait()

    def add_force(comp, tile):
        middle = jnp.zeros((112, 128), jnp.float32)
        turned = jnp.concatenate(
            [from_low_y[comp, tile], middle, from_high_y[comp, tile]], axis=0
        ).T
        part = pl.ds(4 * tile, 4)
        force[comp, part] = core[comp, part] + turned.reshape(4, 32, 128)

    tiles(3, add_force)
    force_up = send(2, force.at[:, 17:19], from_low_x, up_x)
    force_down = send(3, force.at[:, 0:1], from_high_x, down_x)

    def finish(x, extra):
        for comp in range(3):
            total = second[comp, x - 1] + (force[comp, x] + extra(comp))
            final[comp, x - 1] = total
            rim[comp, x] = total.astype(jnp.bfloat16)

    def middle_rows(x, carry):
        finish(x, lambda comp: 0.0)
        return carry

    lax.fori_loop(3, 16, middle_rows, 0)
    force_up.wait()
    force_down.wait()
    finish(1, lambda comp: from_low_x[comp, 0])
    finish(2, lambda comp: from_low_x[comp, 1])
    finish(16, lambda comp: from_high_x[comp, 0])
    rim_x_up = send(4, rim.at[:, 16:17], rim.at[:, 0:1], up_x)
    rim_x_down = send(5, rim.at[:, 1:3], rim.at[:, 17:19], down_x)
    rim_x_up.wait()
    rim_x_down.wait()

    def turn_rim(comp, tile):
        turned = rim[comp, pl.ds(4 * tile, 4)].astype(jnp.float32).reshape(128, 128).T
        rim_down[comp, tile] = turned[0:8]
        rim_up[comp, tile] = turned[120:128]

    tiles(3, turn_rim)
    rim_y_up = send(6, rim_up, rim_low, up_y)
    rim_y_down = send(7, rim_down, rim_high, down_y)
    for comp in range(3):
        field[comp, :, :, 0:128] = rim[comp]
    rim_y_up.wait()
    rim_y_down.wait()

    def fill_field(comp, tile):
        rest = jnp.zeros((112, 128), jnp.float32)
        turned = jnp.concatenate([rim_high[comp, tile], rim_low[comp, tile], rest], axis=0).T
        field[comp, pl.ds(4 * tile, 4), :, 128:256] = turned.reshape(4, 32, 128).astype(
            jnp.bfloat16
        )

    tiles(3, fill_field)


def ghosts(comps):
    return pltpu.VMEM((comps, 5, 8, 128), jnp.float32)


def flow(stacked):
    vmem = pl.BlockSpec(memory_space=pltpu.VMEM)
    return pl.pallas_call(
        functools.partial(flow_kernel, lax.axis_size("gx"), lax.axis_size("gy")),
        in_specs=[vmem],
        out_specs=vmem,
        out_shape=jax.ShapeDtypeStruct((3, 16, 32, 128), jnp.float32),
        scratch_shapes=[
            pltpu.VMEM((4, 20, 32, 256), jnp.float32),
            pltpu.VMEM((3, 18, 32, 256), jnp.float32),
            ghosts(4),
            ghosts(4),
            ghosts(4),
            ghosts(4),
            pltpu.SemaphoreType.DMA((4,)),
            pltpu.SemaphoreType.DMA((4,)),
        ],
        compiler_params=pltpu.CompilerParams(
            collective_id=1, has_side_effects=True, vmem_limit_bytes=32 * 2**20
        ),
        cost_estimate=pl.CostEstimate(
            flops=10**7, bytes_accessed=4 * 10**7, transcendentals=0
        ),
        name="flow",
    )(stacked)


def settle(second, core, above, below):
    vmem = pl.BlockSpec(memory_space=pltpu.VMEM)
    return pl.pallas_call(
        functools.partial(settle_kernel, lax.axis_size("gx"), lax.axis_size("gy")),
        in_specs=[vmem] * 4,
        out_specs=[vmem] * 2,
        out_shape=[
            jax.ShapeDtypeStruct((3, 16, 32, 128), jnp.float32),
            jax.ShapeDtypeStruct((3, 20, 32, 256), jnp.bfloat16),
        ],
        scratch_shapes=[
            pltpu.VMEM((3, 20, 32, 128), jnp.float32),
            pltpu.VMEM((3, 20, 32, 128), jnp.bfloat16),
            ghosts(3),
            ghosts(3),
            pltpu.VMEM((3, 2, 32, 128), jnp.float32),
            pltpu.VMEM((3, 1, 32, 128), jnp.float32),
            ghosts(3),
            ghosts(3),
            ghosts(3),
            ghosts(3),
            pltpu.SemaphoreType.DMA((8,)),
            pltpu.SemaphoreType.DMA((8,)),
        ],
        compiler_params=pltpu.CompilerParams(
            collective_id=0, has_side_effects=True, vmem_limit_bytes=32 * 2**20
        ),
        name="settle",
    )(second, core, above, below)


def body(velocity, viscosity, marker_cells, marker_offset, marker_force):
    depth, width_x, width_y = velocity.shape[1:]
    blocks, _, markers = marker_cells.shape
    column_size = lax.axis_size("gy")
    slots = column_size * CAP
    steps = slots // GROUP

    target = marker_cells[:, 1, 0] // width_y
    same = target[:, None] == target[None, :]
    earlier = jnp.tril(jnp.ones((blocks, blocks), jnp.bool_), -1)
    rank = jnp.sum(jnp.where(same & earlier, 1, 0), axis=1)
    slot_of = target * CAP + rank
    place = (lax.broadcasted_iota(jnp.int32, (slots, blocks), 0) == slot_of[None, :]).astype(
        jnp.float32
    )
    local = jnp.stack(
        [
            marker_cells[:, 0] - lax.axis_index("gx") * width_x,
            marker_cells[:, 1] - target[:, None] * width_y,
            marker_cells[:, 2],
        ],
        axis=1,
    )
    packed = jnp.concatenate([local.astype(jnp.float32), marker_offset, marker_force], axis=1)
    sent = jnp.dot(place, packed.reshape(blocks, -1), precision=lax.Precision.HIGHEST)
    sent = sent.reshape(column_size, CAP * 9, markers)
    received = lax.all_to_all(sent, "gy", 0, 0, tiled=True)
    received = jnp.moveaxis(received.reshape(slots, 9, markers), 1, 0)
    cells = received[0:3].astype(jnp.int32)
    weights = jnp.stack(
        [peskin_weight(shift - received[3 + d]) for d in range(3) for shift in OFFSETS]
    )
    forces = received[6:9]

    rows = XR * depth
    lanes = GROUP * markers
    core, above, below, y_matrix, x_matrix, z_matrix = pl.pallas_call(
        spread_kernel,
        grid=(steps,),
        in_specs=[
            pl.BlockSpec(memory_space=pltpu.VMEM),
            pl.BlockSpec(memory_space=pltpu.VMEM),
            pl.BlockSpec(memory_space=pltpu.VMEM),
        ],
        out_specs=[
            pl.BlockSpec((3, 640, 128), lambda g: (0, 0, 0)),
            pl.BlockSpec((3, 5, 8, 128), lambda g: (0, 0, 0, 0)),
            pl.BlockSpec((3, 5, 8, 128), lambda g: (0, 0, 0, 0)),
            pl.BlockSpec((1, YR, lanes), lambda g: (g, 0, 0)),
            pl.BlockSpec((1, 24, lanes), lambda g: (g, 0, 0)),
            pl.BlockSpec((1, depth, lanes), lambda g: (g, 0, 0)),
        ],
        out_shape=[
            jax.ShapeDtypeStruct((3, 640, 128), jnp.float32),
            jax.ShapeDtypeStruct((3, 5, 8, 128), jnp.float32),
            jax.ShapeDtypeStruct((3, 5, 8, 128), jnp.float32),
            jax.ShapeDtypeStruct((steps, YR, lanes), jnp.bfloat16),
            jax.ShapeDtypeStruct((steps, 24, lanes), jnp.float32),
            jax.ShapeDtypeStruct((steps, depth, lanes), jnp.float32),
        ],
        scratch_shapes=[
            pltpu.VMEM((rows, lanes), jnp.bfloat16),
            pltpu.VMEM((3, 640, 256), jnp.float32),
        ],
        compiler_params=pltpu.CompilerParams(vmem_limit_bytes=24 * 2**20),
        name="spread",
    )(
        cells.reshape(3, steps, GROUP, markers),
        weights.reshape(12, steps, GROUP, markers),
        forces.reshape(3, steps, GROUP, markers),
    )

    stacked = jnp.concatenate([velocity, viscosity[None]], axis=0)
    stacked = jnp.swapaxes(stacked, 1, 2)
    second = flow(stacked)
    final, field = settle(second, core.reshape(3, 20, depth, width_y), above, below)
    field = field.reshape(3, 640, 256)

    sampled = pl.pallas_call(
        sample_kernel,
        grid=(steps,),
        in_specs=[
            pl.BlockSpec(memory_space=pltpu.VMEM),
            pl.BlockSpec((1, YR, lanes), lambda g: (g, 0, 0)),
            pl.BlockSpec((1, 24, lanes), lambda g: (g, 0, 0)),
            pl.BlockSpec((1, depth, lanes), lambda g: (g, 0, 0)),
        ],
        out_specs=pl.BlockSpec((GROUP // CAP, CAP * 3, markers), lambda g: (g, 0, 0)),
        out_shape=jax.ShapeDtypeStruct((column_size, CAP * 3, markers), jnp.float32),
        compiler_params=pltpu.CompilerParams(vmem_limit_bytes=24 * 2**20),
        name="sample",
    )(field, y_matrix, x_matrix, z_matrix)
    returned = lax.all_to_all(sampled, "gy", 0, 0, tiled=True).reshape(slots, -1)
    marker_velocity = jnp.dot(place.T, returned, precision=lax.Precision.HIGHEST)
    return (jnp.swapaxes(final, 1, 2), marker_velocity.reshape(blocks, 3, markers))


def solution(mesh):
    in_specs = (
        P(None, None, "gx", "gy"),
        P(None, "gx", "gy"),
        P(("gx", "gy"), None, None),
        P(("gx", "gy"), None, None),
        P(("gx", "gy"), None, None),
    )
    out_specs = (P(None, None, "gx", "gy"), P(("gx", "gy"), None, None))
    return jax.shard_map(body, mesh=mesh, in_specs=in_specs, out_specs=out_specs, check_vma=False)
```

```python
import functools

import jax
import jax.numpy as jnp
from jax import lax
from jax.experimental import pallas as pl
from jax.experimental.pallas import tpu as pltpu
from jax.sharding import PartitionSpec as P

CAP = 2
OFFSETS = (-1, 0, 1, 2)
GROUP = 8
XR = 19
YR = 144


def peskin_weight(distance):
    magnitude = jnp.abs(distance)
    inner = (
        3.0 - 2.0 * magnitude + jnp.sqrt(1.0 + 4.0 * magnitude - 4.0 * magnitude * magnitude)
    ) / 8.0
    outer = (
        5.0 - 2.0 * magnitude - jnp.sqrt(-7.0 + 12.0 * magnitude - 4.0 * magnitude * magnitude)
    ) / 8.0
    return jnp.where(magnitude < 1.0, inner, outer)


def stencil_rows(rows, cell, weights, direction, slot, wrap):
    line = lax.broadcasted_iota(jnp.int32, (rows, cell.shape[1]), 0)
    matrix = jnp.zeros((rows, cell.shape[1]), jnp.float32)
    for place, shift in enumerate(OFFSETS):
        target = cell + shift
        if wrap:
            target = jnp.where(target < 0, rows - 1, target)
        matrix = jnp.where(
            line == target, weights[4 * direction + place, slot : slot + 1, :], matrix
        )
    return matrix


def spread_kernel(
    cells, weights, forces, core, above, below, y_out, x_out, z_out, lifted, total
):
    depth = z_out.shape[1]
    markers = cells.shape[3]
    rows = lifted.shape[0]
    step = pl.program_id(0)
    cells, weights, forces = cells.at[:, step], weights.at[:, step], forces.at[:, step]

    @pl.when(pl.program_id(0) == 0)
    def _():
        total[...] = jnp.zeros_like(total)

    for slot in range(GROUP):
        lanes = slice(slot * markers, (slot + 1) * markers)
        one = slice(slot, slot + 1)
        y_matrix = stencil_rows(YR, cells[1, one, :], weights, 1, slot, True)
        y_out[0, :, lanes] = y_matrix.astype(jnp.bfloat16)
        x_out[0, :, lanes] = stencil_rows(24, cells[0, one, :] + 1, weights, 0, slot, False)
        z_out[0, :, lanes] = stencil_rows(depth, cells[2, one, :], weights, 2, slot, False)
    for comp in range(3):
        for slot in range(GROUP):
            lanes = slice(slot * markers, (slot + 1) * markers)
            scaled = forces[comp, slot : slot + 1, :] * z_out[0, :, lanes]
            for x in range(XR):
                lifted[x * depth : (x + 1) * depth, lanes] = (
                    scaled * x_out[0, x : x + 1, lanes]
                ).astype(jnp.bfloat16)
        total[comp, 0:rows, 0:YR] += lax.dot_general(
            lifted[...], y_out[0], (((1,), (1,)), ((), ())), preferred_element_type=jnp.float32
        )

    @pl.when(pl.program_id(0) == pl.num_programs(0) - 1)
    def _():
        for comp in range(3):
            core[comp] = total[comp, :, 0:128]
            for tile in range(5):
                turned = total[comp, tile * 128 : (tile + 1) * 128, 128:256].T
                above[comp, tile] = turned[0:8]
                below[comp, tile] = turned[8:16]


def sample_kernel(field, y_ref, x_ref, z_ref, out):
    depth = z_ref.shape[1]
    for comp in range(3):
        along_y = jnp.dot(
            field[comp, 0 : XR * depth, 0:YR], y_ref[0], preferred_element_type=jnp.float32
        )
        column = along_y[0:depth] * x_ref[0, 0:1, :]
        for x in range(1, XR):
            column = column + along_y[x * depth : (x + 1) * depth] * x_ref[0, x : x + 1, :]
        result = jnp.sum(column * z_ref[0], axis=0, keepdims=True)
        for slot in range(GROUP):
            row = (slot % CAP) * 3 + comp
            out[slot // CAP, row : row + 1, :] = result[:, slot * 128 : (slot + 1) * 128]


MESH = pl.DeviceIdType.MESH


def neighbours(count_x, count_y):
    me_x, me_y = lax.axis_index("gx"), lax.axis_index("gy")
    up_x = (lax.rem(me_x + 1, count_x), me_y)
    down_x = (lax.rem(me_x + count_x - 1, count_x), me_y)
    up_y = (me_x, lax.rem(me_y + 1, count_y))
    down_y = (me_x, lax.rem(me_y + count_y - 1, count_y))
    return up_x, down_x, up_y, down_y


def greet(devices):
    barrier = pltpu.get_barrier_semaphore()
    for device in devices:
        pl.semaphore_signal(barrier, inc=1, device_id=device, device_id_type=MESH)
    pl.semaphore_wait(barrier, len(devices))


def sender(send_sems, recv_sems):
    def send(number, source, target, device):
        copy = pltpu.make_async_remote_copy(
            src_ref=source,
            dst_ref=target,
            send_sem=send_sems.at[number],
            recv_sem=recv_sems.at[number],
            device_id=device,
            device_id_type=MESH,
        )
        copy.start()
        return copy

    return send


def tiles(comps, body):
    def step(tile, carry):
        for comp in range(comps):
            body(comp, tile)
        return carry

    lax.fori_loop(0, 5, step, 0)


def all_peers(count, body):
    me_x, me_y = lax.axis_index("gx"), lax.axis_index("gy")

    def step(distance, carry):
        peer = lax.rem(me_y + distance, count)
        body(distance, peer, (me_x, peer))
        return carry

    lax.fori_loop(1, count, step, 0)


def exchange_copy(source, target, send_sems, recv_sems, distance, peer, device):
    return pltpu.make_async_remote_copy(
        src_ref=source.at[peer],
        dst_ref=target.at[lax.axis_index("gy")],
        send_sem=send_sems.at[distance],
        recv_sem=recv_sems.at[distance],
        device_id=device,
        device_id_type=MESH,
    )


def return_kernel(count, source, target, send_sems, recv_sems):
    me = lax.axis_index("gy")
    barrier = pltpu.get_barrier_semaphore()

    def greet_peer(distance, peer, device):
        pl.semaphore_signal(barrier, inc=1, device_id=device, device_id_type=MESH)

    def start(*where):
        exchange_copy(source, target, send_sems, recv_sems, *where).start()

    def finish(*where):
        exchange_copy(source, target, send_sems, recv_sems, *where).wait()

    all_peers(count, greet_peer)
    pl.semaphore_wait(barrier, count - 1)
    all_peers(count, start)
    target[me] = source[me]
    all_peers(count, finish)


def send_back(rows):
    count = lax.axis_size("gy")
    vmem = pl.BlockSpec(memory_space=pltpu.VMEM)
    return pl.pallas_call(
        functools.partial(return_kernel, count),
        in_specs=[vmem],
        out_specs=vmem,
        out_shape=jax.ShapeDtypeStruct(rows.shape, rows.dtype),
        scratch_shapes=[pltpu.SemaphoreType.DMA((count,)), pltpu.SemaphoreType.DMA((count,))],
        compiler_params=pltpu.CompilerParams(
            collective_id=2, has_side_effects=True, vmem_limit_bytes=32 * 2**20
        ),
        name="send_back",
    )(rows)


def flow_kernel(
    count_x, count_y, stacked, second, wide, first, to_high, to_low, ghost_low, ghost_high,
    send_sems, recv_sems,
):
    up_x, down_x, up_y, down_y = neighbours(count_x, count_y)
    greet((up_x, down_x, up_y, down_y))
    send = sender(send_sems, recv_sems)
    x_up = send(0, stacked.at[:, 14:16], wide.at[:, 0:2, :, 0:128], up_x)
    x_down = send(1, stacked.at[:, 0:2], wide.at[:, 18:20, :, 0:128], down_x)
    wide[:, 2:18, :, 0:128] = stacked[...]
    x_up.wait()
    x_down.wait()

    def turn_wide(comp, tile):
        turned = wide[comp, pl.ds(4 * tile, 4), :, 0:128].reshape(128, 128).T
        to_low[comp, tile] = turned[0:8]
        to_high[comp, tile] = turned[120:128]

    tiles(4, turn_wide)
    wide_up = send(2, to_high, ghost_low, up_y)
    wide_down = send(3, to_low, ghost_high, down_y)
    wide_up.wait()
    wide_down.wait()

    def fill_wide(comp, tile):
        middle = jnp.zeros((112, 128), jnp.float32)
        turned = jnp.concatenate(
            [ghost_high[comp, tile], middle, ghost_low[comp, tile]], axis=0
        ).T
        wide[comp, pl.ds(4 * tile, 4), :, 128:256] = turned.reshape(4, 32, 128)

    tiles(4, fill_wide)

    height = lax.broadcasted_iota(jnp.int32, (32, 256), 0)

    def relaxed(source, x, visc_x, store):
        visc = wide[3, visc_x]
        low_x = 0.5 * (visc + wide[3, visc_x - 1])
        high_x = 0.5 * (visc + wide[3, visc_x + 1])
        low_y = 0.5 * (visc + pltpu.roll(visc, 1, 1))
        high_y = 0.5 * (visc + pltpu.roll(visc, 255, 1))
        low_z = jnp.where(height > 0, 0.5 * (visc + pltpu.roll(visc, 1, 0)), 0.0)
        high_z = jnp.where(height < 31, 0.5 * (visc + pltpu.roll(visc, 31, 0)), 0.0)
        for comp in range(3):
            here = source[comp, x]
            total = low_x * (source[comp, x - 1] - here)
            total = total + high_x * (source[comp, x + 1] - here)
            total = total + low_y * (pltpu.roll(here, 1, 1) - here)
            total = total + high_y * (pltpu.roll(here, 255, 1) - here)
            total = total + low_z * (pltpu.roll(here, 1, 0) - here)
            total = total + high_z * (pltpu.roll(here, 31, 0) - here)
            store(comp, here + total)

    def first_step(x, carry):
        def store(comp, value):
            first[comp, x - 1] = value

        relaxed(wide, x, x, store)
        return carry

    lax.fori_loop(1, 19, first_step, 0)

    def second_step(x, carry):
        def store(comp, value):
            second[comp, x - 1] = value[:, 0:128]

        relaxed(first, x, x + 1, store)
        return carry

    lax.fori_loop(1, 17, second_step, 0)


def settle_kernel(
    count_x, count_y, second, core, above, below,
    final, field,
    force, rim, from_low_y, from_high_y, from_low_x, from_high_x,
    rim_up, rim_down, rim_low, rim_high, send_sems, recv_sems,
):
    up_x, down_x, up_y, down_y = neighbours(count_x, count_y)
    greet((up_x, down_x, up_y, down_y))
    send = sender(send_sems, recv_sems)
    y_up = send(0, above, from_low_y, up_y)
    y_down = send(1, below, from_high_y, down_y)
    rim[:, 19:20] = jnp.zeros_like(rim[:, 19:20])
    y_up.wait()
    y_down.wait()

    def add_force(comp, tile):
        middle = jnp.zeros((112, 128), jnp.float32)
        turned = jnp.concatenate(
            [from_low_y[comp, tile], middle, from_high_y[comp, tile]], axis=0
        ).T
        part = pl.ds(4 * tile, 4)
        force[comp, part] = core[comp, part] + turned.reshape(4, 32, 128)

    tiles(3, add_force)
    force_up = send(2, force.at[:, 17:19], from_low_x, up_x)
    force_down = send(3, force.at[:, 0:1], from_high_x, down_x)

    def finish(x, extra):
        for comp in range(3):
            total = second[comp, x - 1] + (force[comp, x] + extra(comp))
            final[comp, x - 1] = total
            rim[comp, x] = total.astype(jnp.bfloat16)

    def middle_rows(x, carry):
        finish(x, lambda comp: 0.0)
        return carry

    lax.fori_loop(3, 16, middle_rows, 0)
    force_up.wait()
    force_down.wait()
    finish(1, lambda comp: from_low_x[comp, 0])
    finish(2, lambda comp: from_low_x[comp, 1])
    finish(16, lambda comp: from_high_x[comp, 0])
    rim_x_up = send(4, rim.at[:, 16:17], rim.at[:, 0:1], up_x)
    rim_x_down = send(5, rim.at[:, 1:3], rim.at[:, 17:19], down_x)
    rim_x_up.wait()
    rim_x_down.wait()

    def turn_rim(comp, tile):
        turned = rim[comp, pl.ds(4 * tile, 4)].astype(jnp.float32).reshape(128, 128).T
        rim_down[comp, tile] = turned[0:8]
        rim_up[comp, tile] = turned[120:128]

    tiles(3, turn_rim)
    rim_y_up = send(6, rim_up, rim_low, up_y)
    rim_y_down = send(7, rim_down, rim_high, down_y)
    for comp in range(3):
        field[comp, :, :, 0:128] = rim[comp]
    rim_y_up.wait()
    rim_y_down.wait()

    def fill_field(comp, tile):
        rest = jnp.zeros((112, 128), jnp.float32)
        turned = jnp.concatenate([rim_high[comp, tile], rim_low[comp, tile], rest], axis=0).T
        field[comp, pl.ds(4 * tile, 4), :, 128:256] = turned.reshape(4, 32, 128).astype(
            jnp.bfloat16
        )

    tiles(3, fill_field)


def ghosts(comps):
    return pltpu.VMEM((comps, 5, 8, 128), jnp.float32)


def flow(stacked):
    vmem = pl.BlockSpec(memory_space=pltpu.VMEM)
    return pl.pallas_call(
        functools.partial(flow_kernel, lax.axis_size("gx"), lax.axis_size("gy")),
        in_specs=[vmem],
        out_specs=vmem,
        out_shape=jax.ShapeDtypeStruct((3, 16, 32, 128), jnp.float32),
        scratch_shapes=[
            pltpu.VMEM((4, 20, 32, 256), jnp.float32),
            pltpu.VMEM((3, 18, 32, 256), jnp.float32),
            ghosts(4),
            ghosts(4),
            ghosts(4),
            ghosts(4),
            pltpu.SemaphoreType.DMA((4,)),
            pltpu.SemaphoreType.DMA((4,)),
        ],
        compiler_params=pltpu.CompilerParams(
            collective_id=1, has_side_effects=True, vmem_limit_bytes=32 * 2**20
        ),
        cost_estimate=pl.CostEstimate(
            flops=10**7, bytes_accessed=4 * 10**7, transcendentals=0
        ),
        name="flow",
    )(stacked)


def settle(second, core, above, below):
    vmem = pl.BlockSpec(memory_space=pltpu.VMEM)
    return pl.pallas_call(
        functools.partial(settle_kernel, lax.axis_size("gx"), lax.axis_size("gy")),
        in_specs=[vmem] * 4,
        out_specs=[vmem] * 2,
        out_shape=[
            jax.ShapeDtypeStruct((3, 16, 32, 128), jnp.float32),
            jax.ShapeDtypeStruct((3, 20, 32, 256), jnp.bfloat16),
        ],
        scratch_shapes=[
            pltpu.VMEM((3, 20, 32, 128), jnp.float32),
            pltpu.VMEM((3, 20, 32, 128), jnp.bfloat16),
            ghosts(3),
            ghosts(3),
            pltpu.VMEM((3, 2, 32, 128), jnp.float32),
            pltpu.VMEM((3, 1, 32, 128), jnp.float32),
            ghosts(3),
            ghosts(3),
            ghosts(3),
            ghosts(3),
            pltpu.SemaphoreType.DMA((8,)),
            pltpu.SemaphoreType.DMA((8,)),
        ],
        compiler_params=pltpu.CompilerParams(
            collective_id=0, has_side_effects=True, vmem_limit_bytes=32 * 2**20
        ),
        name="settle",
    )(second, core, above, below)


def body(velocity, viscosity, marker_cells, marker_offset, marker_force):
    depth, width_x, width_y = velocity.shape[1:]
    blocks, _, markers = marker_cells.shape
    column_size = lax.axis_size("gy")
    slots = column_size * CAP
    steps = slots // GROUP

    target = marker_cells[:, 1, 0] // width_y
    same = target[:, None] == target[None, :]
    earlier = jnp.tril(jnp.ones((blocks, blocks), jnp.bool_), -1)
    rank = jnp.sum(jnp.where(same & earlier, 1, 0), axis=1)
    slot_of = target * CAP + rank
    place = (lax.broadcasted_iota(jnp.int32, (slots, blocks), 0) == slot_of[None, :]).astype(
        jnp.float32
    )
    local = jnp.stack(
        [
            marker_cells[:, 0] - lax.axis_index("gx") * width_x,
            marker_cells[:, 1] - target[:, None] * width_y,
            marker_cells[:, 2],
        ],
        axis=1,
    )
    packed = jnp.concatenate([local.astype(jnp.float32), marker_offset, marker_force], axis=1)
    sent = jnp.dot(place, packed.reshape(blocks, -1), precision=lax.Precision.HIGHEST)
    sent = sent.reshape(column_size, CAP * 9, markers)
    received = lax.all_to_all(sent, "gy", 0, 0, tiled=True)
    received = jnp.moveaxis(received.reshape(slots, 9, markers), 1, 0)
    cells = received[0:3].astype(jnp.int32)
    weights = jnp.stack(
        [peskin_weight(shift - received[3 + d]) for d in range(3) for shift in OFFSETS]
    )
    forces = received[6:9]

    rows = XR * depth
    lanes = GROUP * markers
    core, above, below, y_matrix, x_matrix, z_matrix = pl.pallas_call(
        spread_kernel,
        grid=(steps,),
        in_specs=[
            pl.BlockSpec(memory_space=pltpu.VMEM),
            pl.BlockSpec(memory_space=pltpu.VMEM),
            pl.BlockSpec(memory_space=pltpu.VMEM),
        ],
        out_specs=[
            pl.BlockSpec((3, 640, 128), lambda g: (0, 0, 0)),
            pl.BlockSpec((3, 5, 8, 128), lambda g: (0, 0, 0, 0)),
            pl.BlockSpec((3, 5, 8, 128), lambda g: (0, 0, 0, 0)),
            pl.BlockSpec((1, YR, lanes), lambda g: (g, 0, 0)),
            pl.BlockSpec((1, 24, lanes), lambda g: (g, 0, 0)),
            pl.BlockSpec((1, depth, lanes), lambda g: (g, 0, 0)),
        ],
        out_shape=[
            jax.ShapeDtypeStruct((3, 640, 128), jnp.float32),
            jax.ShapeDtypeStruct((3, 5, 8, 128), jnp.float32),
            jax.ShapeDtypeStruct((3, 5, 8, 128), jnp.float32),
            jax.ShapeDtypeStruct((steps, YR, lanes), jnp.bfloat16),
            jax.ShapeDtypeStruct((steps, 24, lanes), jnp.float32),
            jax.ShapeDtypeStruct((steps, depth, lanes), jnp.float32),
        ],
        scratch_shapes=[
            pltpu.VMEM((rows, lanes), jnp.bfloat16),
            pltpu.VMEM((3, 640, 256), jnp.float32),
        ],
        compiler_params=pltpu.CompilerParams(vmem_limit_bytes=24 * 2**20),
        name="spread",
    )(
        cells.reshape(3, steps, GROUP, markers),
        weights.reshape(12, steps, GROUP, markers),
        forces.reshape(3, steps, GROUP, markers),
    )

    stacked = jnp.concatenate([velocity, viscosity[None]], axis=0)
    stacked = jnp.swapaxes(stacked, 1, 2)
    second = flow(stacked)
    final, field = settle(second, core.reshape(3, 20, depth, width_y), above, below)
    field = field.reshape(3, 640, 256)

    sampled = pl.pallas_call(
        sample_kernel,
        grid=(steps,),
        in_specs=[
            pl.BlockSpec(memory_space=pltpu.VMEM),
            pl.BlockSpec((1, YR, lanes), lambda g: (g, 0, 0)),
            pl.BlockSpec((1, 24, lanes), lambda g: (g, 0, 0)),
            pl.BlockSpec((1, depth, lanes), lambda g: (g, 0, 0)),
        ],
        out_specs=pl.BlockSpec((GROUP // CAP, CAP * 3, markers), lambda g: (g, 0, 0)),
        out_shape=jax.ShapeDtypeStruct((column_size, CAP * 3, markers), jnp.float32),
        compiler_params=pltpu.CompilerParams(vmem_limit_bytes=24 * 2**20),
        name="sample",
    )(field, y_matrix, x_matrix, z_matrix)
    returned = send_back(sampled).reshape(slots, -1)
    marker_velocity = jnp.dot(place.T, returned, precision=lax.Precision.HIGHEST)
    return (jnp.swapaxes(final, 1, 2), marker_velocity.reshape(blocks, 3, markers))


def solution(mesh):
    in_specs = (
        P(None, None, "gx", "gy"),
        P(None, "gx", "gy"),
        P(("gx", "gy"), None, None),
        P(("gx", "gy"), None, None),
        P(("gx", "gy"), None, None),
    )
    out_specs = (P(None, None, "gx", "gy"), P(("gx", "gy"), None, None))
    return jax.shard_map(body, mesh=mesh, in_specs=in_specs, out_specs=out_specs, check_vma=False)
```

```python
import functools

import jax
import jax.numpy as jnp
from jax import lax
from jax.experimental import pallas as pl
from jax.experimental.pallas import tpu as pltpu
from jax.sharding import PartitionSpec as P

CAP = 2
OFFSETS = (-1, 0, 1, 2)
GROUP = 8
XR = 19
YR = 144


def peskin_weight(distance):
    magnitude = jnp.abs(distance)
    inner = (
        3.0 - 2.0 * magnitude + jnp.sqrt(1.0 + 4.0 * magnitude - 4.0 * magnitude * magnitude)
    ) / 8.0
    outer = (
        5.0 - 2.0 * magnitude - jnp.sqrt(-7.0 + 12.0 * magnitude - 4.0 * magnitude * magnitude)
    ) / 8.0
    return jnp.where(magnitude < 1.0, inner, outer)


def stencil_rows(rows, cell, weights, direction, slot, wrap):
    line = lax.broadcasted_iota(jnp.int32, (rows, cell.shape[1]), 0)
    matrix = jnp.zeros((rows, cell.shape[1]), jnp.float32)
    for place, shift in enumerate(OFFSETS):
        target = cell + shift
        if wrap:
            target = jnp.where(target < 0, rows - 1, target)
        matrix = jnp.where(
            line == target, weights[4 * direction + place, slot : slot + 1, :], matrix
        )
    return matrix


def spread_kernel(
    cells, weights, forces, core, above, below, y_out, x_out, z_out, lifted, total
):
    depth = z_out.shape[1]
    markers = cells.shape[3]
    rows = lifted.shape[0]
    step = pl.program_id(0)
    cells, weights, forces = cells.at[:, step], weights.at[:, step], forces.at[:, step]

    @pl.when(pl.program_id(0) == 0)
    def _():
        total[...] = jnp.zeros_like(total)

    for slot in range(GROUP):
        lanes = slice(slot * markers, (slot + 1) * markers)
        one = slice(slot, slot + 1)
        y_matrix = stencil_rows(YR, cells[1, one, :], weights, 1, slot, True)
        y_out[0, :, lanes] = y_matrix.astype(jnp.bfloat16)
        x_out[0, :, lanes] = stencil_rows(24, cells[0, one, :] + 1, weights, 0, slot, False)
        z_out[0, :, lanes] = stencil_rows(depth, cells[2, one, :], weights, 2, slot, False)
    for comp in range(3):
        for slot in range(GROUP):
            lanes = slice(slot * markers, (slot + 1) * markers)
            scaled = forces[comp, slot : slot + 1, :] * z_out[0, :, lanes]
            for x in range(XR):
                lifted[x * depth : (x + 1) * depth, lanes] = (
                    scaled * x_out[0, x : x + 1, lanes]
                ).astype(jnp.bfloat16)
        total[comp, 0:rows, 0:YR] += lax.dot_general(
            lifted[...], y_out[0], (((1,), (1,)), ((), ())), preferred_element_type=jnp.float32
        )

    @pl.when(pl.program_id(0) == pl.num_programs(0) - 1)
    def _():
        for comp in range(3):
            core[comp] = total[comp, :, 0:128]
            for tile in range(5):
                turned = total[comp, tile * 128 : (tile + 1) * 128, 128:256].T
                above[comp, tile] = turned[0:8]
                below[comp, tile] = turned[8:16]


def sample_kernel(field, y_ref, x_ref, z_ref, out):
    depth = z_ref.shape[1]
    for comp in range(3):
        along_y = jnp.dot(
            field[comp, 0 : XR * depth, 0:YR], y_ref[0], preferred_element_type=jnp.float32
        )
        column = along_y[0:depth] * x_ref[0, 0:1, :]
        for x in range(1, XR):
            column = column + along_y[x * depth : (x + 1) * depth] * x_ref[0, x : x + 1, :]
        result = jnp.sum(column * z_ref[0], axis=0, keepdims=True)
        for slot in range(GROUP):
            row = (slot % CAP) * 3 + comp
            out[slot // CAP, row : row + 1, :] = result[:, slot * 128 : (slot + 1) * 128]


MESH = pl.DeviceIdType.MESH


def neighbours(count_x, count_y):
    me_x, me_y = lax.axis_index("gx"), lax.axis_index("gy")
    up_x = (lax.rem(me_x + 1, count_x), me_y)
    down_x = (lax.rem(me_x + count_x - 1, count_x), me_y)
    up_y = (me_x, lax.rem(me_y + 1, count_y))
    down_y = (me_x, lax.rem(me_y + count_y - 1, count_y))
    return up_x, down_x, up_y, down_y


def greet(devices):
    barrier = pltpu.get_barrier_semaphore()
    for device in devices:
        pl.semaphore_signal(barrier, inc=1, device_id=device, device_id_type=MESH)
    pl.semaphore_wait(barrier, len(devices))


def sender(send_sems, recv_sems):
    def send(number, source, target, device):
        copy = pltpu.make_async_remote_copy(
            src_ref=source,
            dst_ref=target,
            send_sem=send_sems.at[number],
            recv_sem=recv_sems.at[number],
            device_id=device,
            device_id_type=MESH,
        )
        copy.start()
        return copy

    return send


def tiles(comps, body):
    def step(tile, carry):
        for comp in range(comps):
            body(comp, tile)
        return carry

    lax.fori_loop(0, 5, step, 0)


def all_peers(count, body):
    me_x, me_y = lax.axis_index("gx"), lax.axis_index("gy")

    def step(distance, carry):
        peer = lax.rem(me_y + distance, count)
        body(distance, peer, (me_x, peer))
        return carry

    lax.fori_loop(1, count, step, 0)


def exchange_copy(source, target, send_sems, recv_sems, distance, peer, device):
    return pltpu.make_async_remote_copy(
        src_ref=source.at[peer],
        dst_ref=target.at[lax.axis_index("gy")],
        send_sem=send_sems.at[distance],
        recv_sem=recv_sems.at[distance],
        device_id=device,
        device_id_type=MESH,
    )


def return_kernel(count, source, target, send_sems, recv_sems):
    me = lax.axis_index("gy")
    barrier = pltpu.get_barrier_semaphore()

    def greet_peer(distance, peer, device):
        pl.semaphore_signal(barrier, inc=1, device_id=device, device_id_type=MESH)

    def start(*where):
        exchange_copy(source, target, send_sems, recv_sems, *where).start()

    def finish(*where):
        exchange_copy(source, target, send_sems, recv_sems, *where).wait()

    all_peers(count, greet_peer)
    pl.semaphore_wait(barrier, count - 1)
    all_peers(count, start)
    target[me] = source[me]
    all_peers(count, finish)


def send_back(rows):
    count = lax.axis_size("gy")
    vmem = pl.BlockSpec(memory_space=pltpu.VMEM)
    return pl.pallas_call(
        functools.partial(return_kernel, count),
        in_specs=[vmem],
        out_specs=vmem,
        out_shape=jax.ShapeDtypeStruct(rows.shape, rows.dtype),
        scratch_shapes=[pltpu.SemaphoreType.DMA((count,)), pltpu.SemaphoreType.DMA((count,))],
        compiler_params=pltpu.CompilerParams(
            collective_id=2, has_side_effects=True, vmem_limit_bytes=32 * 2**20
        ),
        name="send_back",
    )(rows)


def flow_kernel(
    count_x, count_y, stacked, sent, second, received,
    wide, first, to_high, to_low, ghost_low, ghost_high,
    send_sems, recv_sems, block_send_sems, block_recv_sems,
):
    me = lax.axis_index("gy")
    up_x, down_x, up_y, down_y = neighbours(count_x, count_y)
    barrier = pltpu.get_barrier_semaphore()

    def greet_peer(distance, peer, device):
        pl.semaphore_signal(barrier, inc=1, device_id=device, device_id_type=MESH)

    def start_block(*where):
        exchange_copy(sent, received, block_send_sems, block_recv_sems, *where).start()

    def finish_block(*where):
        exchange_copy(sent, received, block_send_sems, block_recv_sems, *where).wait()

    for device in (up_x, down_x):
        pl.semaphore_signal(barrier, inc=1, device_id=device, device_id_type=MESH)
    all_peers(count_y, greet_peer)
    pl.semaphore_wait(barrier, count_y + 1)
    send = sender(send_sems, recv_sems)
    x_up = send(0, stacked.at[:, 14:16], wide.at[:, 0:2, :, 0:128], up_x)
    x_down = send(1, stacked.at[:, 0:2], wide.at[:, 18:20, :, 0:128], down_x)
    all_peers(count_y, start_block)
    received[me] = sent[me]
    wide[:, 2:18, :, 0:128] = stacked[...]
    x_up.wait()
    x_down.wait()

    def turn_wide(comp, tile):
        turned = wide[comp, pl.ds(4 * tile, 4), :, 0:128].reshape(128, 128).T
        to_low[comp, tile] = turned[0:8]
        to_high[comp, tile] = turned[120:128]

    tiles(4, turn_wide)
    wide_up = send(2, to_high, ghost_low, up_y)
    wide_down = send(3, to_low, ghost_high, down_y)
    wide_up.wait()
    wide_down.wait()

    def fill_wide(comp, tile):
        middle = jnp.zeros((112, 128), jnp.float32)
        turned = jnp.concatenate(
            [ghost_high[comp, tile], middle, ghost_low[comp, tile]], axis=0
        ).T
        wide[comp, pl.ds(4 * tile, 4), :, 128:256] = turned.reshape(4, 32, 128)

    tiles(4, fill_wide)

    height = lax.broadcasted_iota(jnp.int32, (32, 256), 0)

    def relaxed(source, x, visc_x, store):
        visc = wide[3, visc_x]
        low_x = 0.5 * (visc + wide[3, visc_x - 1])
        high_x = 0.5 * (visc + wide[3, visc_x + 1])
        low_y = 0.5 * (visc + pltpu.roll(visc, 1, 1))
        high_y = 0.5 * (visc + pltpu.roll(visc, 255, 1))
        low_z = jnp.where(height > 0, 0.5 * (visc + pltpu.roll(visc, 1, 0)), 0.0)
        high_z = jnp.where(height < 31, 0.5 * (visc + pltpu.roll(visc, 31, 0)), 0.0)
        for comp in range(3):
            here = source[comp, x]
            total = low_x * (source[comp, x - 1] - here)
            total = total + high_x * (source[comp, x + 1] - here)
            total = total + low_y * (pltpu.roll(here, 1, 1) - here)
            total = total + high_y * (pltpu.roll(here, 255, 1) - here)
            total = total + low_z * (pltpu.roll(here, 1, 0) - here)
            total = total + high_z * (pltpu.roll(here, 31, 0) - here)
            store(comp, here + total)

    def first_step(x, carry):
        def store(comp, value):
            first[comp, x - 1] = value

        relaxed(wide, x, x, store)
        return carry

    lax.fori_loop(1, 19, first_step, 0)

    def second_step(x, carry):
        def store(comp, value):
            second[comp, x - 1] = value[:, 0:128]

        relaxed(first, x, x + 1, store)
        return carry

    lax.fori_loop(1, 17, second_step, 0)
    all_peers(count_y, finish_block)


def settle_kernel(
    count_x, count_y, second, core, above, below,
    final, field,
    force, rim, from_low_y, from_high_y, from_low_x, from_high_x,
    rim_up, rim_down, rim_low, rim_high, send_sems, recv_sems,
):
    up_x, down_x, up_y, down_y = neighbours(count_x, count_y)
    greet((up_x, down_x, up_y, down_y))
    send = sender(send_sems, recv_sems)
    y_up = send(0, above, from_low_y, up_y)
    y_down = send(1, below, from_high_y, down_y)
    rim[:, 19:20] = jnp.zeros_like(rim[:, 19:20])
    y_up.wait()
    y_down.wait()

    def add_force(comp, tile):
        middle = jnp.zeros((112, 128), jnp.float32)
        turned = jnp.concatenate(
            [from_low_y[comp, tile], middle, from_high_y[comp, tile]], axis=0
        ).T
        part = pl.ds(4 * tile, 4)
        force[comp, part] = core[comp, part] + turned.reshape(4, 32, 128)

    tiles(3, add_force)
    force_up = send(2, force.at[:, 17:19], from_low_x, up_x)
    force_down = send(3, force.at[:, 0:1], from_high_x, down_x)

    def finish(x, extra):
        for comp in range(3):
            total = second[comp, x - 1] + (force[comp, x] + extra(comp))
            final[comp, x - 1] = total
            rim[comp, x] = total.astype(jnp.bfloat16)

    def middle_rows(x, carry):
        finish(x, lambda comp: 0.0)
        return carry

    lax.fori_loop(3, 16, middle_rows, 0)
    force_up.wait()
    force_down.wait()
    finish(1, lambda comp: from_low_x[comp, 0])
    finish(2, lambda comp: from_low_x[comp, 1])
    finish(16, lambda comp: from_high_x[comp, 0])
    rim_x_up = send(4, rim.at[:, 16:17], rim.at[:, 0:1], up_x)
    rim_x_down = send(5, rim.at[:, 1:3], rim.at[:, 17:19], down_x)
    rim_x_up.wait()
    rim_x_down.wait()

    def turn_rim(comp, tile):
        turned = rim[comp, pl.ds(4 * tile, 4)].astype(jnp.float32).reshape(128, 128).T
        rim_down[comp, tile] = turned[0:8]
        rim_up[comp, tile] = turned[120:128]

    tiles(3, turn_rim)
    rim_y_up = send(6, rim_up, rim_low, up_y)
    rim_y_down = send(7, rim_down, rim_high, down_y)
    for comp in range(3):
        field[comp, :, :, 0:128] = rim[comp]
    rim_y_up.wait()
    rim_y_down.wait()

    def fill_field(comp, tile):
        rest = jnp.zeros((112, 128), jnp.float32)
        turned = jnp.concatenate([rim_high[comp, tile], rim_low[comp, tile], rest], axis=0).T
        field[comp, pl.ds(4 * tile, 4), :, 128:256] = turned.reshape(4, 32, 128).astype(
            jnp.bfloat16
        )

    tiles(3, fill_field)


def ghosts(comps):
    return pltpu.VMEM((comps, 5, 8, 128), jnp.float32)


def flow(stacked, sent):
    count_y = lax.axis_size("gy")
    vmem = pl.BlockSpec(memory_space=pltpu.VMEM)
    return pl.pallas_call(
        functools.partial(flow_kernel, lax.axis_size("gx"), count_y),
        in_specs=[vmem] * 2,
        out_specs=[vmem] * 2,
        out_shape=[
            jax.ShapeDtypeStruct((3, 16, 32, 128), jnp.float32),
            jax.ShapeDtypeStruct(sent.shape, sent.dtype),
        ],
        scratch_shapes=[
            pltpu.VMEM((4, 20, 32, 256), jnp.float32),
            pltpu.VMEM((3, 18, 32, 256), jnp.float32),
            ghosts(4),
            ghosts(4),
            ghosts(4),
            ghosts(4),
            pltpu.SemaphoreType.DMA((4,)),
            pltpu.SemaphoreType.DMA((4,)),
            pltpu.SemaphoreType.DMA((count_y,)),
            pltpu.SemaphoreType.DMA((count_y,)),
        ],
        compiler_params=pltpu.CompilerParams(
            collective_id=1, has_side_effects=True, vmem_limit_bytes=32 * 2**20
        ),
        cost_estimate=pl.CostEstimate(
            flops=10**7, bytes_accessed=4 * 10**7, transcendentals=0
        ),
        name="flow",
    )(stacked, sent)


def settle(second, core, above, below):
    vmem = pl.BlockSpec(memory_space=pltpu.VMEM)
    return pl.pallas_call(
        functools.partial(settle_kernel, lax.axis_size("gx"), lax.axis_size("gy")),
        in_specs=[vmem] * 4,
        out_specs=[vmem] * 2,
        out_shape=[
            jax.ShapeDtypeStruct((3, 16, 32, 128), jnp.float32),
            jax.ShapeDtypeStruct((3, 20, 32, 256), jnp.bfloat16),
        ],
        scratch_shapes=[
            pltpu.VMEM((3, 20, 32, 128), jnp.float32),
            pltpu.VMEM((3, 20, 32, 128), jnp.bfloat16),
            ghosts(3),
            ghosts(3),
            pltpu.VMEM((3, 2, 32, 128), jnp.float32),
            pltpu.VMEM((3, 1, 32, 128), jnp.float32),
            ghosts(3),
            ghosts(3),
            ghosts(3),
            ghosts(3),
            pltpu.SemaphoreType.DMA((8,)),
            pltpu.SemaphoreType.DMA((8,)),
        ],
        compiler_params=pltpu.CompilerParams(
            collective_id=0, has_side_effects=True, vmem_limit_bytes=32 * 2**20
        ),
        name="settle",
    )(second, core, above, below)


def body(velocity, viscosity, marker_cells, marker_offset, marker_force):
    depth, width_x, width_y = velocity.shape[1:]
    blocks, _, markers = marker_cells.shape
    column_size = lax.axis_size("gy")
    slots = column_size * CAP
    steps = slots // GROUP

    target = marker_cells[:, 1, 0] // width_y
    same = target[:, None] == target[None, :]
    earlier = jnp.tril(jnp.ones((blocks, blocks), jnp.bool_), -1)
    rank = jnp.sum(jnp.where(same & earlier, 1, 0), axis=1)
    slot_of = target * CAP + rank
    place = (lax.broadcasted_iota(jnp.int32, (slots, blocks), 0) == slot_of[None, :]).astype(
        jnp.float32
    )
    local = jnp.stack(
        [
            marker_cells[:, 0] - lax.axis_index("gx") * width_x,
            marker_cells[:, 1] - target[:, None] * width_y,
            marker_cells[:, 2],
        ],
        axis=1,
    )
    packed = jnp.concatenate([local.astype(jnp.float32), marker_offset, marker_force], axis=1)
    sent = jnp.dot(place, packed.reshape(blocks, -1), precision=lax.Precision.HIGHEST)
    sent = sent.reshape(column_size, CAP * 9, markers)
    stacked = jnp.concatenate([velocity, viscosity[None]], axis=0)
    stacked = jnp.swapaxes(stacked, 1, 2)
    second, received = flow(stacked, sent)
    received = jnp.moveaxis(received.reshape(slots, 9, markers), 1, 0)
    cells = received[0:3].astype(jnp.int32)
    weights = jnp.stack(
        [peskin_weight(shift - received[3 + d]) for d in range(3) for shift in OFFSETS]
    )
    forces = received[6:9]

    rows = XR * depth
    lanes = GROUP * markers
    core, above, below, y_matrix, x_matrix, z_matrix = pl.pallas_call(
        spread_kernel,
        grid=(steps,),
        in_specs=[
            pl.BlockSpec(memory_space=pltpu.VMEM),
            pl.BlockSpec(memory_space=pltpu.VMEM),
            pl.BlockSpec(memory_space=pltpu.VMEM),
        ],
        out_specs=[
            pl.BlockSpec((3, 640, 128), lambda g: (0, 0, 0)),
            pl.BlockSpec((3, 5, 8, 128), lambda g: (0, 0, 0, 0)),
            pl.BlockSpec((3, 5, 8, 128), lambda g: (0, 0, 0, 0)),
            pl.BlockSpec((1, YR, lanes), lambda g: (g, 0, 0)),
            pl.BlockSpec((1, 24, lanes), lambda g: (g, 0, 0)),
            pl.BlockSpec((1, depth, lanes), lambda g: (g, 0, 0)),
        ],
        out_shape=[
            jax.ShapeDtypeStruct((3, 640, 128), jnp.float32),
            jax.ShapeDtypeStruct((3, 5, 8, 128), jnp.float32),
            jax.ShapeDtypeStruct((3, 5, 8, 128), jnp.float32),
            jax.ShapeDtypeStruct((steps, YR, lanes), jnp.bfloat16),
            jax.ShapeDtypeStruct((steps, 24, lanes), jnp.float32),
            jax.ShapeDtypeStruct((steps, depth, lanes), jnp.float32),
        ],
        scratch_shapes=[
            pltpu.VMEM((rows, lanes), jnp.bfloat16),
            pltpu.VMEM((3, 640, 256), jnp.float32),
        ],
        compiler_params=pltpu.CompilerParams(vmem_limit_bytes=24 * 2**20),
        name="spread",
    )(
        cells.reshape(3, steps, GROUP, markers),
        weights.reshape(12, steps, GROUP, markers),
        forces.reshape(3, steps, GROUP, markers),
    )

    final, field = settle(second, core.reshape(3, 20, depth, width_y), above, below)
    field = field.reshape(3, 640, 256)

    sampled = pl.pallas_call(
        sample_kernel,
        grid=(steps,),
        in_specs=[
            pl.BlockSpec(memory_space=pltpu.VMEM),
            pl.BlockSpec((1, YR, lanes), lambda g: (g, 0, 0)),
            pl.BlockSpec((1, 24, lanes), lambda g: (g, 0, 0)),
            pl.BlockSpec((1, depth, lanes), lambda g: (g, 0, 0)),
        ],
        out_specs=pl.BlockSpec((GROUP // CAP, CAP * 3, markers), lambda g: (g, 0, 0)),
        out_shape=jax.ShapeDtypeStruct((column_size, CAP * 3, markers), jnp.float32),
        compiler_params=pltpu.CompilerParams(vmem_limit_bytes=24 * 2**20),
        name="sample",
    )(field, y_matrix, x_matrix, z_matrix)
    returned = send_back(sampled).reshape(slots, -1)
    marker_velocity = jnp.dot(place.T, returned, precision=lax.Precision.HIGHEST)
    return (jnp.swapaxes(final, 1, 2), marker_velocity.reshape(blocks, 3, markers))


def solution(mesh):
    in_specs = (
        P(None, None, "gx", "gy"),
        P(None, "gx", "gy"),
        P(("gx", "gy"), None, None),
        P(("gx", "gy"), None, None),
        P(("gx", "gy"), None, None),
    )
    out_specs = (P(None, None, "gx", "gy"), P(("gx", "gy"), None, None))
    return jax.shard_map(body, mesh=mesh, in_specs=in_specs, out_specs=out_specs, check_vma=False)
```

```python
import functools

import jax
import jax.numpy as jnp
from jax import lax
from jax.experimental import pallas as pl
from jax.experimental.pallas import tpu as pltpu
from jax.sharding import PartitionSpec as P

CAP = 2
OFFSETS = (-1, 0, 1, 2)
GROUP = 8
XR = 19
YR = 144


def peskin_weight(distance):
    magnitude = jnp.abs(distance)
    inner = (
        3.0 - 2.0 * magnitude + jnp.sqrt(1.0 + 4.0 * magnitude - 4.0 * magnitude * magnitude)
    ) / 8.0
    outer = (
        5.0 - 2.0 * magnitude - jnp.sqrt(-7.0 + 12.0 * magnitude - 4.0 * magnitude * magnitude)
    ) / 8.0
    return jnp.where(magnitude < 1.0, inner, outer)


def stencil_rows(rows, cell, weights, direction, slot, wrap):
    line = lax.broadcasted_iota(jnp.int32, (rows, cell.shape[1]), 0)
    matrix = jnp.zeros((rows, cell.shape[1]), jnp.float32)
    for place, shift in enumerate(OFFSETS):
        target = cell + shift
        if wrap:
            target = jnp.where(target < 0, rows - 1, target)
        matrix = jnp.where(
            line == target, weights[4 * direction + place, slot : slot + 1, :], matrix
        )
    return matrix


def spread_kernel(
    cells, weights, forces, core, above, below, y_out, x_out, z_out, lifted, total
):
    depth = z_out.shape[1]
    markers = cells.shape[3]
    rows = lifted.shape[0]
    step = pl.program_id(0)
    cells, weights, forces = cells.at[:, step], weights.at[:, step], forces.at[:, step]

    @pl.when(pl.program_id(0) == 0)
    def _():
        total[...] = jnp.zeros_like(total)

    for slot in range(GROUP):
        lanes = slice(slot * markers, (slot + 1) * markers)
        one = slice(slot, slot + 1)
        y_matrix = stencil_rows(YR, cells[1, one, :], weights, 1, slot, True)
        y_out[0, :, lanes] = y_matrix.astype(jnp.bfloat16)
        x_out[0, :, lanes] = stencil_rows(24, cells[0, one, :] + 1, weights, 0, slot, False)
        z_out[0, :, lanes] = stencil_rows(depth, cells[2, one, :], weights, 2, slot, False)
    for comp in range(3):
        for slot in range(GROUP):
            lanes = slice(slot * markers, (slot + 1) * markers)
            scaled = forces[comp, slot : slot + 1, :] * z_out[0, :, lanes]
            for x in range(XR):
                lifted[x * depth : (x + 1) * depth, lanes] = (
                    scaled * x_out[0, x : x + 1, lanes]
                ).astype(jnp.bfloat16)
        total[comp, 0:rows, 0:YR] += lax.dot_general(
            lifted[...], y_out[0], (((1,), (1,)), ((), ())), preferred_element_type=jnp.float32
        )

    @pl.when(pl.program_id(0) == pl.num_programs(0) - 1)
    def _():
        for comp in range(3):
            core[comp] = total[comp, :, 0:128]
            for tile in range(5):
                turned = total[comp, tile * 128 : (tile + 1) * 128, 128:256].T
                above[comp, tile] = turned[0:8]
                below[comp, tile] = turned[8:16]


def sample_kernel(field, y_ref, x_ref, z_ref, out):
    depth = z_ref.shape[1]
    for comp in range(3):
        along_y = jnp.dot(
            field[comp, 0 : XR * depth, 0:YR], y_ref[0], preferred_element_type=jnp.float32
        )
        column = along_y[0:depth] * x_ref[0, 0:1, :]
        for x in range(1, XR):
            column = column + along_y[x * depth : (x + 1) * depth] * x_ref[0, x : x + 1, :]
        result = jnp.sum(column * z_ref[0], axis=0, keepdims=True)
        for slot in range(GROUP):
            row = (slot % CAP) * 3 + comp
            out[slot // CAP, row : row + 1, :] = result[:, slot * 128 : (slot + 1) * 128]


MESH = pl.DeviceIdType.MESH


def neighbours(count_x, count_y):
    me_x, me_y = lax.axis_index("gx"), lax.axis_index("gy")
    up_x = (lax.rem(me_x + 1, count_x), me_y)
    down_x = (lax.rem(me_x + count_x - 1, count_x), me_y)
    up_y = (me_x, lax.rem(me_y + 1, count_y))
    down_y = (me_x, lax.rem(me_y + count_y - 1, count_y))
    return up_x, down_x, up_y, down_y


def greet(devices):
    barrier = pltpu.get_barrier_semaphore()
    for device in devices:
        pl.semaphore_signal(barrier, inc=1, device_id=device, device_id_type=MESH)
    pl.semaphore_wait(barrier, len(devices))


def sender(send_sems, recv_sems):
    def send(number, source, target, device):
        copy = pltpu.make_async_remote_copy(
            src_ref=source,
            dst_ref=target,
            send_sem=send_sems.at[number],
            recv_sem=recv_sems.at[number],
            device_id=device,
            device_id_type=MESH,
        )
        copy.start()
        return copy

    return send


def tiles(comps, body):
    def step(tile, carry):
        for comp in range(comps):
            body(comp, tile)
        return carry

    lax.fori_loop(0, 5, step, 0)


def all_peers(count, body):
    me_x, me_y = lax.axis_index("gx"), lax.axis_index("gy")

    def step(distance, carry):
        peer = lax.rem(me_y + distance, count)
        body(distance, peer, (me_x, peer))
        return carry

    lax.fori_loop(1, count, step, 0)


def exchange_copy(source, target, send_sems, recv_sems, distance, peer, device):
    return pltpu.make_async_remote_copy(
        src_ref=source.at[peer],
        dst_ref=target.at[lax.axis_index("gy")],
        send_sem=send_sems.at[distance],
        recv_sem=recv_sems.at[distance],
        device_id=device,
        device_id_type=MESH,
    )


def return_kernel(count, source, target, send_sems, recv_sems):
    me = lax.axis_index("gy")
    barrier = pltpu.get_barrier_semaphore()

    def greet_peer(distance, peer, device):
        pl.semaphore_signal(barrier, inc=1, device_id=device, device_id_type=MESH)

    def start(*where):
        exchange_copy(source, target, send_sems, recv_sems, *where).start()

    def finish(*where):
        exchange_copy(source, target, send_sems, recv_sems, *where).wait()

    all_peers(count, greet_peer)
    pl.semaphore_wait(barrier, count - 1)
    all_peers(count, start)
    target[me] = source[me]
    all_peers(count, finish)


def send_back(rows):
    count = lax.axis_size("gy")
    vmem = pl.BlockSpec(memory_space=pltpu.VMEM)
    return pl.pallas_call(
        functools.partial(return_kernel, count),
        in_specs=[vmem],
        out_specs=vmem,
        out_shape=jax.ShapeDtypeStruct(rows.shape, rows.dtype),
        scratch_shapes=[pltpu.SemaphoreType.DMA((count,)), pltpu.SemaphoreType.DMA((count,))],
        compiler_params=pltpu.CompilerParams(
            collective_id=2, has_side_effects=True, vmem_limit_bytes=32 * 2**20
        ),
        name="send_back",
    )(rows)


def flow_kernel(
    count_x, count_y, stacked, sent, second, received,
    wide, first, to_high, to_low, ghost_low, ghost_high,
    send_sems, recv_sems, block_send_sems, block_recv_sems,
):
    me = lax.axis_index("gy")
    up_x, down_x, up_y, down_y = neighbours(count_x, count_y)
    barrier = pltpu.get_barrier_semaphore()

    def greet_peer(distance, peer, device):
        pl.semaphore_signal(barrier, inc=1, device_id=device, device_id_type=MESH)

    def start_block(*where):
        exchange_copy(sent, received, block_send_sems, block_recv_sems, *where).start()

    def finish_block(*where):
        exchange_copy(sent, received, block_send_sems, block_recv_sems, *where).wait()

    for device in (up_x, down_x):
        pl.semaphore_signal(barrier, inc=1, device_id=device, device_id_type=MESH)
    all_peers(count_y, greet_peer)
    pl.semaphore_wait(barrier, count_y + 1)
    send = sender(send_sems, recv_sems)
    x_up = send(0, stacked.at[:, 14:16], wide.at[:, 0:2, :, 0:128], up_x)
    x_down = send(1, stacked.at[:, 0:2], wide.at[:, 18:20, :, 0:128], down_x)
    wide[:, 2:18, :, 0:128] = stacked[...]
    x_up.wait()
    x_down.wait()

    def turn_wide(comp, tile):
        turned = wide[comp, pl.ds(4 * tile, 4), :, 0:128].reshape(128, 128).T
        to_low[comp, tile] = turned[0:8]
        to_high[comp, tile] = turned[120:128]

    tiles(4, turn_wide)
    wide_up = send(2, to_high, ghost_low, up_y)
    wide_down = send(3, to_low, ghost_high, down_y)
    all_peers(count_y, start_block)
    received[me] = sent[me]
    wide_up.wait()
    wide_down.wait()

    def fill_wide(comp, tile):
        middle = jnp.zeros((112, 128), jnp.float32)
        turned = jnp.concatenate(
            [ghost_high[comp, tile], middle, ghost_low[comp, tile]], axis=0
        ).T
        wide[comp, pl.ds(4 * tile, 4), :, 128:256] = turned.reshape(4, 32, 128)

    tiles(4, fill_wide)

    height = lax.broadcasted_iota(jnp.int32, (32, 256), 0)

    def relaxed(source, x, visc_x, store):
        visc = wide[3, visc_x]
        low_x = 0.5 * (visc + wide[3, visc_x - 1])
        high_x = 0.5 * (visc + wide[3, visc_x + 1])
        low_y = 0.5 * (visc + pltpu.roll(visc, 1, 1))
        high_y = 0.5 * (visc + pltpu.roll(visc, 255, 1))
        low_z = jnp.where(height > 0, 0.5 * (visc + pltpu.roll(visc, 1, 0)), 0.0)
        high_z = jnp.where(height < 31, 0.5 * (visc + pltpu.roll(visc, 31, 0)), 0.0)
        for comp in range(3):
            here = source[comp, x]
            total = low_x * (source[comp, x - 1] - here)
            total = total + high_x * (source[comp, x + 1] - here)
            total = total + low_y * (pltpu.roll(here, 1, 1) - here)
            total = total + high_y * (pltpu.roll(here, 255, 1) - here)
            total = total + low_z * (pltpu.roll(here, 1, 0) - here)
            total = total + high_z * (pltpu.roll(here, 31, 0) - here)
            store(comp, here + total)

    def first_step(x, carry):
        def store(comp, value):
            first[comp, x - 1] = value

        relaxed(wide, x, x, store)
        return carry

    lax.fori_loop(1, 19, first_step, 0)

    def second_step(x, carry):
        def store(comp, value):
            second[comp, x - 1] = value[:, 0:128]

        relaxed(first, x, x + 1, store)
        return carry

    lax.fori_loop(1, 17, second_step, 0)
    all_peers(count_y, finish_block)


def settle_kernel(
    count_x, count_y, second, core, above, below,
    final, field,
    force, rim, from_low_y, from_high_y, from_low_x, from_high_x,
    rim_up, rim_down, rim_low, rim_high, send_sems, recv_sems,
):
    up_x, down_x, up_y, down_y = neighbours(count_x, count_y)
    greet((up_x, down_x, up_y, down_y))
    send = sender(send_sems, recv_sems)
    y_up = send(0, above, from_low_y, up_y)
    y_down = send(1, below, from_high_y, down_y)
    rim[:, 19:20] = jnp.zeros_like(rim[:, 19:20])
    y_up.wait()
    y_down.wait()

    def add_force(comp, tile):
        middle = jnp.zeros((112, 128), jnp.float32)
        turned = jnp.concatenate(
            [from_low_y[comp, tile], middle, from_high_y[comp, tile]], axis=0
        ).T
        part = pl.ds(4 * tile, 4)
        force[comp, part] = core[comp, part] + turned.reshape(4, 32, 128)

    tiles(3, add_force)
    force_up = send(2, force.at[:, 17:19], from_low_x, up_x)
    force_down = send(3, force.at[:, 0:1], from_high_x, down_x)

    def finish(x, extra):
        for comp in range(3):
            total = second[comp, x - 1] + (force[comp, x] + extra(comp))
            final[comp, x - 1] = total
            rim[comp, x] = total.astype(jnp.bfloat16)

    def middle_rows(x, carry):
        finish(x, lambda comp: 0.0)
        return carry

    lax.fori_loop(3, 16, middle_rows, 0)
    force_up.wait()
    force_down.wait()
    finish(1, lambda comp: from_low_x[comp, 0])
    finish(2, lambda comp: from_low_x[comp, 1])
    finish(16, lambda comp: from_high_x[comp, 0])
    rim_x_up = send(4, rim.at[:, 16:17], rim.at[:, 0:1], up_x)
    rim_x_down = send(5, rim.at[:, 1:3], rim.at[:, 17:19], down_x)
    rim_x_up.wait()
    rim_x_down.wait()

    def turn_rim(comp, tile):
        turned = rim[comp, pl.ds(4 * tile, 4)].astype(jnp.float32).reshape(128, 128).T
        rim_down[comp, tile] = turned[0:8]
        rim_up[comp, tile] = turned[120:128]

    tiles(3, turn_rim)
    rim_y_up = send(6, rim_up, rim_low, up_y)
    rim_y_down = send(7, rim_down, rim_high, down_y)
    for comp in range(3):
        field[comp, :, :, 0:128] = rim[comp]
    rim_y_up.wait()
    rim_y_down.wait()

    def fill_field(comp, tile):
        rest = jnp.zeros((112, 128), jnp.float32)
        turned = jnp.concatenate([rim_high[comp, tile], rim_low[comp, tile], rest], axis=0).T
        field[comp, pl.ds(4 * tile, 4), :, 128:256] = turned.reshape(4, 32, 128).astype(
            jnp.bfloat16
        )

    tiles(3, fill_field)


def ghosts(comps):
    return pltpu.VMEM((comps, 5, 8, 128), jnp.float32)


def flow(stacked, sent):
    count_y = lax.axis_size("gy")
    vmem = pl.BlockSpec(memory_space=pltpu.VMEM)
    return pl.pallas_call(
        functools.partial(flow_kernel, lax.axis_size("gx"), count_y),
        in_specs=[vmem] * 2,
        out_specs=[vmem] * 2,
        out_shape=[
            jax.ShapeDtypeStruct((3, 16, 32, 128), jnp.float32),
            jax.ShapeDtypeStruct(sent.shape, sent.dtype),
        ],
        scratch_shapes=[
            pltpu.VMEM((4, 20, 32, 256), jnp.float32),
            pltpu.VMEM((3, 18, 32, 256), jnp.float32),
            ghosts(4),
            ghosts(4),
            ghosts(4),
            ghosts(4),
            pltpu.SemaphoreType.DMA((4,)),
            pltpu.SemaphoreType.DMA((4,)),
            pltpu.SemaphoreType.DMA((count_y,)),
            pltpu.SemaphoreType.DMA((count_y,)),
        ],
        compiler_params=pltpu.CompilerParams(
            collective_id=1, has_side_effects=True, vmem_limit_bytes=32 * 2**20
        ),
        cost_estimate=pl.CostEstimate(
            flops=10**7, bytes_accessed=4 * 10**7, transcendentals=0
        ),
        name="flow",
    )(stacked, sent)


def settle(second, core, above, below):
    vmem = pl.BlockSpec(memory_space=pltpu.VMEM)
    return pl.pallas_call(
        functools.partial(settle_kernel, lax.axis_size("gx"), lax.axis_size("gy")),
        in_specs=[vmem] * 4,
        out_specs=[vmem] * 2,
        out_shape=[
            jax.ShapeDtypeStruct((3, 16, 32, 128), jnp.float32),
            jax.ShapeDtypeStruct((3, 20, 32, 256), jnp.bfloat16),
        ],
        scratch_shapes=[
            pltpu.VMEM((3, 20, 32, 128), jnp.float32),
            pltpu.VMEM((3, 20, 32, 128), jnp.bfloat16),
            ghosts(3),
            ghosts(3),
            pltpu.VMEM((3, 2, 32, 128), jnp.float32),
            pltpu.VMEM((3, 1, 32, 128), jnp.float32),
            ghosts(3),
            ghosts(3),
            ghosts(3),
            ghosts(3),
            pltpu.SemaphoreType.DMA((8,)),
            pltpu.SemaphoreType.DMA((8,)),
        ],
        compiler_params=pltpu.CompilerParams(
            collective_id=0, has_side_effects=True, vmem_limit_bytes=32 * 2**20
        ),
        name="settle",
    )(second, core, above, below)


def body(velocity, viscosity, marker_cells, marker_offset, marker_force):
    depth, width_x, width_y = velocity.shape[1:]
    blocks, _, markers = marker_cells.shape
    column_size = lax.axis_size("gy")
    slots = column_size * CAP
    steps = slots // GROUP

    target = marker_cells[:, 1, 0] // width_y
    same = target[:, None] == target[None, :]
    earlier = jnp.tril(jnp.ones((blocks, blocks), jnp.bool_), -1)
    rank = jnp.sum(jnp.where(same & earlier, 1, 0), axis=1)
    slot_of = target * CAP + rank
    place = (lax.broadcasted_iota(jnp.int32, (slots, blocks), 0) == slot_of[None, :]).astype(
        jnp.float32
    )
    local = jnp.stack(
        [
            marker_cells[:, 0] - lax.axis_index("gx") * width_x,
            marker_cells[:, 1] - target[:, None] * width_y,
            marker_cells[:, 2],
        ],
        axis=1,
    )
    packed = jnp.concatenate([local.astype(jnp.float32), marker_offset, marker_force], axis=1)
    sent = jnp.dot(place, packed.reshape(blocks, -1), precision=lax.Precision.HIGHEST)
    sent = sent.reshape(column_size, CAP * 9, markers)
    stacked = jnp.concatenate([velocity, viscosity[None]], axis=0)
    stacked = jnp.swapaxes(stacked, 1, 2)
    second, received = flow(stacked, sent)
    received = jnp.moveaxis(received.reshape(slots, 9, markers), 1, 0)
    cells = received[0:3].astype(jnp.int32)
    weights = jnp.stack(
        [peskin_weight(shift - received[3 + d]) for d in range(3) for shift in OFFSETS]
    )
    forces = received[6:9]

    rows = XR * depth
    lanes = GROUP * markers
    core, above, below, y_matrix, x_matrix, z_matrix = pl.pallas_call(
        spread_kernel,
        grid=(steps,),
        in_specs=[
            pl.BlockSpec(memory_space=pltpu.VMEM),
            pl.BlockSpec(memory_space=pltpu.VMEM),
            pl.BlockSpec(memory_space=pltpu.VMEM),
        ],
        out_specs=[
            pl.BlockSpec((3, 640, 128), lambda g: (0, 0, 0)),
            pl.BlockSpec((3, 5, 8, 128), lambda g: (0, 0, 0, 0)),
            pl.BlockSpec((3, 5, 8, 128), lambda g: (0, 0, 0, 0)),
            pl.BlockSpec((1, YR, lanes), lambda g: (g, 0, 0)),
            pl.BlockSpec((1, 24, lanes), lambda g: (g, 0, 0)),
            pl.BlockSpec((1, depth, lanes), lambda g: (g, 0, 0)),
        ],
        out_shape=[
            jax.ShapeDtypeStruct((3, 640, 128), jnp.float32),
            jax.ShapeDtypeStruct((3, 5, 8, 128), jnp.float32),
            jax.ShapeDtypeStruct((3, 5, 8, 128), jnp.float32),
            jax.ShapeDtypeStruct((steps, YR, lanes), jnp.bfloat16),
            jax.ShapeDtypeStruct((steps, 24, lanes), jnp.float32),
            jax.ShapeDtypeStruct((steps, depth, lanes), jnp.float32),
        ],
        scratch_shapes=[
            pltpu.VMEM((rows, lanes), jnp.bfloat16),
            pltpu.VMEM((3, 640, 256), jnp.float32),
        ],
        compiler_params=pltpu.CompilerParams(vmem_limit_bytes=24 * 2**20),
        name="spread",
    )(
        cells.reshape(3, steps, GROUP, markers),
        weights.reshape(12, steps, GROUP, markers),
        forces.reshape(3, steps, GROUP, markers),
    )

    final, field = settle(second, core.reshape(3, 20, depth, width_y), above, below)
    field = field.reshape(3, 640, 256)

    sampled = pl.pallas_call(
        sample_kernel,
        grid=(steps,),
        in_specs=[
            pl.BlockSpec(memory_space=pltpu.VMEM),
            pl.BlockSpec((1, YR, lanes), lambda g: (g, 0, 0)),
            pl.BlockSpec((1, 24, lanes), lambda g: (g, 0, 0)),
            pl.BlockSpec((1, depth, lanes), lambda g: (g, 0, 0)),
        ],
        out_specs=pl.BlockSpec((GROUP // CAP, CAP * 3, markers), lambda g: (g, 0, 0)),
        out_shape=jax.ShapeDtypeStruct((column_size, CAP * 3, markers), jnp.float32),
        compiler_params=pltpu.CompilerParams(vmem_limit_bytes=24 * 2**20),
        name="sample",
    )(field, y_matrix, x_matrix, z_matrix)
    returned = send_back(sampled).reshape(slots, -1)
    marker_velocity = jnp.dot(place.T, returned, precision=lax.Precision.HIGHEST)
    return (jnp.swapaxes(final, 1, 2), marker_velocity.reshape(blocks, 3, markers))


def solution(mesh):
    in_specs = (
        P(None, None, "gx", "gy"),
        P(None, "gx", "gy"),
        P(("gx", "gy"), None, None),
        P(("gx", "gy"), None, None),
        P(("gx", "gy"), None, None),
    )
    out_specs = (P(None, None, "gx", "gy"), P(("gx", "gy"), None, None))
    return jax.shard_map(body, mesh=mesh, in_specs=in_specs, out_specs=out_specs, check_vma=False)
```
